256 devices in a mesh: node: 64 (over z, y, core), state: 4 (over x).
Axes of the slice: x: 4, y: 4, z: 8, core: 2. Of those that a mesh axis runs over, the one named last changes fastest.
Arguments:
- block: bfloat16 [64, 2097152], P('state', 'node'), may hold values from -6 to 6
- connectivity: int32 [125, 32768], P(None, 'node'), may hold values from 0 to 49151, as said below
- potential: float32 [125, 32768], P(None, 'node'), may hold values from 0.1 to 3
- cell_matrix: bfloat16 [125, 125], replicated, as said below
Outputs:
- orthonormal: bfloat16 [64, 2097152], P('state', 'node')
- factor: float32 [64, 64], replicated
The draws below stay inside these ranges and needn't reach their ends.
Inputs may be any that keep to these rules, and one draw needn't show every extreme that they name: `connectivity`: in each slab, numbers below 8192 are the previous slab's last 8192 nodes and numbers from 40960 on are the next slab's first nodes. The numbers of the slab's k-th cell (k from 0) lie in k * 96 to k * 96 + 2 * 96 - 1, those of its last cell in k * 96 to k * 96 + 95; each cell reaches the lower end of its range. `cell_matrix`: Symmetric.
All inputs are finite; a program needn't handle non-finite values.
Results may differ from the reference program's by a relative error of at most 0.015.
Values may be sent and summed in bfloat16 or wider, within the bound.
No kernel may reach another device: no remote copies, remote signals or barrier semaphores. Data moves between devices by JAX's collectives and lax.ppermute only.
A program may use at most 64 MiB of HBM per device.

```python
import math
import jax
import jax.numpy as jnp
from jax import lax

NSTATE = 64
CELL_NODES = 125
SEG = 96
CELL_DEV = 512
NODE_DEV = 32768
BND = 8192
EXT = 49152
NODES = 2097152
CELLS = 32768
N_NODE = 64


def draw_connectivity(key, part):
    offsets = jax.random.randint(key, (CELL_NODES, CELLS), 0, 2 * SEG, dtype=jnp.int32)
    column = jnp.arange(CELLS, dtype=jnp.int32) % CELL_DEV
    last = column == CELL_DEV - 1
    offsets = jnp.where(last[None, :], offsets % SEG, offsets)
    base = column * SEG
    links = offsets + base[None, :]
    links = links.at[0, :].set(base)
    top = jnp.where(last, base + SEG - 1, base + 2 * SEG - 1)
    links = links.at[CELL_NODES - 1, :].set(top)
    return links


def draw_cell_matrix(key, part):
    noise = jax.random.normal(key, (CELL_NODES, CELL_NODES), jnp.float32) * (0.5 / CELL_NODES ** 0.5)
    symmetric = (noise + noise.T) * 0.5
    return (symmetric + jnp.eye(CELL_NODES, dtype=jnp.float32)).astype(jnp.bfloat16)


def level_of(stream_key, dims, pieces, low, largest):
    gain = 1.0
    for position, parts in pieces:
        heights = jax.random.uniform(jax.random.fold_in(jax.random.fold_in(stream_key, 6), position), (parts,), jnp.float32, low / len(pieces), largest / len(pieces))
        gain = gain * jnp.repeat(jnp.exp(heights), dims[position] // parts).reshape((-1,) + (1,) * (len(dims) - 1 - position))
    return gain


def scatter_about(key, extent, spread, most, shards=(), kind=jnp.bfloat16):
    result = spread * jax.random.normal(key, extent, jnp.float32)
    if shards:
        result = result * level_of(key, extent, shards, -0.22, 0.18)
    return jnp.clip(result, -most, most).astype(kind)


def setup_inputs(seed: int = 0) -> dict:
    seeds = jax.random.split(jax.random.key(seed), 5)
    block = scatter_about(seeds[0], (NSTATE, NODES), 1.0, 6.0, ((0, 4), (1, 64)))
    connectivity = draw_connectivity(jax.random.fold_in(seeds[4], 71), 0)
    potential = jnp.clip(jnp.exp(math.log(3.0) - 3.4011974 * jax.random.uniform(seeds[2], (CELL_NODES, CELLS), jnp.float32) ** level_of(seeds[2], (CELL_NODES, CELLS), ((1, 64),), -0.2, 0.2)), 0.1, 3.0)
    cell_matrix = draw_cell_matrix(jax.random.fold_in(seeds[4], 71), 0)
    return dict(block=block, connectivity=connectivity, potential=potential, cell_matrix=cell_matrix)


def cell_terms(window, connectivity, potential, cell_matrix):
    states = window.shape[0]
    values = window[:, connectivity].astype(jnp.float32)
    mixed = jnp.einsum('ij,sjc->sic', cell_matrix.astype(jnp.float32), values)
    mixed = mixed + potential[None] * values
    summed = jnp.zeros((states, window.shape[1]), jnp.float32)
    return summed.at[:, connectivity.reshape(-1)].add(mixed.reshape(states, -1))

def apply_hamiltonian(field, connectivity, potential, cell_matrix):
    nodes = field.shape[1]
    padded = jnp.pad(field, ((0, 0), (BND, BND)))

    def one_slab(total, slab):
        window = lax.dynamic_slice_in_dim(padded, slab * NODE_DEV, EXT, 1)
        links = lax.dynamic_slice_in_dim(connectivity, slab * CELL_DEV, CELL_DEV, 1)
        local = lax.dynamic_slice_in_dim(potential, slab * CELL_DEV, CELL_DEV, 1)
        contrib = cell_terms(window, links, local, cell_matrix)
        current = lax.dynamic_slice_in_dim(total, slab * NODE_DEV, EXT, 1)
        total = lax.dynamic_update_slice_in_dim(total, current + contrib, slab * NODE_DEV, 1)
        return (total, None)
    total = jnp.zeros((field.shape[0], nodes + 2 * BND), jnp.float32)
    total, unused = lax.scan(one_slab, total, jnp.arange(N_NODE, dtype=jnp.int32))
    return total[:, BND:BND + nodes]

def reference(block, connectivity, potential, cell_matrix):
    start = block.astype(jnp.float32)
    image = apply_hamiltonian(block, connectivity, potential, cell_matrix)
    first = ((image - 3.0 * start) / 3.0).astype(jnp.bfloat16)
    image = apply_hamiltonian(first, connectivity, potential, cell_matrix)
    second = (2.0 * (image - 3.0 * first.astype(jnp.float32)) / 3.0 - start).astype(jnp.bfloat16)
    intersection = jnp.dot(second.astype(jnp.float32), second.T.astype(jnp.float32), preferred_element_type=jnp.float32) / NODES
    factor = jnp.linalg.cholesky(intersection)
    identity = jnp.eye(NSTATE, dtype=factor.dtype)
    inverse = lax.linalg.triangular_solve(factor, identity, left_side=True, lower=True).astype(jnp.bfloat16)
    orthonormal = jnp.dot(inverse.astype(jnp.float32), second.astype(jnp.float32), preferred_element_type=jnp.float32).astype(jnp.bfloat16)
    return (orthonormal, factor)
```

```python
import functools

import jax
import jax.numpy as jnp
from jax import lax
from jax.experimental import pallas as pl
from jax.experimental.pallas import tpu as pltpu
from jax.sharding import PartitionSpec as P

CENTER = 3.0
HALF_WIDTH = 3.0
LANE = 128
QUAD = 4
HALO = 6
UNROLL = 2
ABSENT = 1024
CELL_TILES = ((0, 1), (0, 1, 2), (1, 2), (2, 3))


def floor_div3(x):
    return (x + 999) // 3 - 333


def ranges(slot, low, high, tiles, edge, slots):
    groups = slots * tiles // 2

    def clip(origin, first, last):
        start = jnp.maximum(-floor_div3(origin - low), first)
        stop = jnp.minimum(floor_div3(high - origin), last)
        return start, origin + 3 * start, jnp.maximum(stop - start + 1, 0)

    own = clip(-edge - tiles * slot, 0, groups - 1)
    before = slot < slots // 2
    origin = jnp.where(
        before, -edge - slots * tiles - tiles * slot, slots * tiles - edge - tiles * slot
    )
    other = clip(origin, 0, groups - 1)
    shift = jnp.where(before, groups - 24, 0)
    return own, (other[0] - shift, other[1], other[2])


def operator_kernel(
    slots, tiles, edge, window_ref, own_ref, other_ref, matrix_ref, second_ref, gram_ref, field, acc
):
    slot = lax.axis_index("state")
    slab = lax.axis_index("node")
    slabs = lax.axis_size("node")
    states, width = window_ref.shape
    full = acc.shape[1]
    owned = tiles * LANE
    margin = HALO * LANE
    rows = lax.broadcasted_iota(jnp.int32, (LANE, LANE), 0).astype(jnp.float32)

    def sweep(source, cells_ref, first, tile, count):
        def body(step, carry):
            base = tile + HALO + 3 * UNROLL * step
            column = pl.multiple_of(base * LANE, LANE)
            out = [None] * (3 * UNROLL + 1)
            for part in range(UNROLL):
                at = pl.multiple_of(column + 3 * part * LANE, LANE)
                x = source[:, pl.ds(at, 4 * LANE)]
                line = QUAD * (first + UNROLL * step + part)
                pickers, values, values_half = [], [], []
                for cell in range(QUAD):
                    node = cells_ref[0, pl.ds(line + cell, 1), :]
                    picked = [
                        (rows == node + (96.0 * cell - 128.0 * t + ABSENT)).astype(jnp.bfloat16)
                        for t in CELL_TILES[cell]
                    ]
                    pickers.append(dict(zip(CELL_TILES[cell], picked)))
                    begin = CELL_TILES[cell][0] * LANE
                    end = (CELL_TILES[cell][-1] + 1) * LANE
                    value = jnp.dot(
                        x[:, begin:end],
                        jnp.concatenate(picked, axis=0),
                        preferred_element_type=jnp.float32,
                    )
                    values.append(value)
                    values_half.append(value.astype(jnp.bfloat16))
                mixed = jnp.dot(
                    jnp.concatenate(values_half, axis=0),
                    matrix_ref[...],
                    preferred_element_type=jnp.float32,
                )
                mixed_half = []
                for cell in range(QUAD):
                    level = cells_ref[1, pl.ds(line + cell, 1), :]
                    term = mixed[states * cell : states * (cell + 1)] + level * values[cell]
                    mixed_half.append(term.astype(jnp.bfloat16))
                for t in range(4):
                    cells = [c for c in range(QUAD) if t in CELL_TILES[c]]
                    spread = lax.dot_general(
                        jnp.concatenate([mixed_half[c] for c in cells], axis=1),
                        jnp.concatenate([pickers[c][t] for c in cells], axis=1),
                        (((1,), (1,)), ((), ())),
                        preferred_element_type=jnp.float32,
                    )
                    k = 3 * part + t
                    out[k] = spread if out[k] is None else out[k] + spread
            for k, spread in enumerate(out):
                at = pl.multiple_of(column + k * LANE, LANE)
                acc[:, pl.ds(at, LANE)] += spread
            return carry

        lax.fori_loop(0, (count + UNROLL - 1) // UNROLL, body, 0)

    def apply(source, low, high):
        own, other = ranges(slot, low, high, tiles, edge, slots)
        sweep(source, own_ref, *own)
        sweep(source, other_ref, *other)

    field[:, pl.ds(0, width)] = window_ref[...]
    field[:, pl.ds(width, full - width)] = jnp.zeros((states, full - width), field.dtype)
    acc[...] = jnp.zeros_like(acc)
    apply(field, -HALO, tiles + 2)

    def to_first(step, carry):
        at = pl.multiple_of(step * 2 * LANE, 2 * LANE)
        here = pl.ds(at, 2 * LANE)
        start = window_ref[:, here].astype(jnp.float32)
        field[:, here] = ((acc[:, here] - CENTER * start) / HALF_WIDTH).astype(field.dtype)
        acc[:, here] = jnp.zeros((states, 2 * LANE), jnp.float32)
        return carry

    lax.fori_loop(0, width // (2 * LANE), to_first, 0)

    @pl.when((slab == 0) & (slot == 0))
    def _():
        field[:, pl.ds(0, margin)] = jnp.zeros((states, margin), field.dtype)

    @pl.when((slab == slabs - 1) & (slot == slots - 1))
    def _():
        field[:, pl.ds(margin + owned, margin)] = jnp.zeros((states, margin), field.dtype)

    apply(field, -3, tiles - 1)

    def to_second(step, gram):
        at = pl.multiple_of(step * 4 * LANE, 4 * LANE)
        here = pl.ds(pl.multiple_of(at + margin, 2 * LANE), 4 * LANE)
        image = acc[:, here] - CENTER * field[:, here].astype(jnp.float32)
        start = window_ref[:, here].astype(jnp.float32)
        second = (2.0 * image / HALF_WIDTH - start).astype(second_ref.dtype)
        second_ref[:, pl.ds(at, 4 * LANE)] = second
        return gram + lax.dot_general(
            second, second, (((1,), (1,)), ((), ())), preferred_element_type=jnp.float32
        )

    gram_ref[...] = lax.fori_loop(
        0, owned // (4 * LANE), to_second, jnp.zeros((states, states), jnp.float32)
    )


def filtered(window, own, other, matrix, slots, tiles, edge):
    states, width = window.shape
    full = width + (3 * UNROLL + 1) * LANE
    return pl.pallas_call(
        functools.partial(operator_kernel, slots, tiles, edge),
        out_shape=(
            jax.ShapeDtypeStruct((states, tiles * LANE), window.dtype),
            jax.ShapeDtypeStruct((states, states), jnp.float32),
        ),
        in_specs=[pl.BlockSpec(memory_space=pltpu.VMEM)] * 4,
        out_specs=[pl.BlockSpec(memory_space=pltpu.VMEM)] * 2,
        scratch_shapes=[
            pltpu.VMEM((states, full), window.dtype),
            pltpu.VMEM((states, full), jnp.float32),
        ],
        compiler_params=pltpu.CompilerParams(vmem_limit_bytes=40 << 20),
        name="operator",
    )(window, own, other, matrix)


def exchanged_sum(x):
    slabs = lax.axis_size("node")
    for stride in (1, 8):
        if stride == 1:
            groups = [[8 * g + i for i in range(8)] for g in range(slabs // 8)]
        else:
            groups = [[g + 8 * i for i in range(slabs // 8)] for g in range(8)]
        copies = jnp.broadcast_to(x[None], (len(groups[0]), *x.shape))
        x = lax.all_to_all(copies, "node", 0, 0, axis_index_groups=groups).sum(0)
    copies = jnp.broadcast_to(x[None], (lax.axis_size("state"), *x.shape))
    return lax.all_to_all(copies, "state", 0, 0).sum(0)


def factorize(intersection):
    factor = jnp.linalg.cholesky(intersection)
    identity = jnp.eye(intersection.shape[0], dtype=factor.dtype)
    inverse = lax.linalg.triangular_solve(factor, identity, left_side=True, lower=True).astype(
        jnp.bfloat16
    )
    return (factor, inverse)


def per_device(block, connectivity, potential, cell_matrix):
    rows, owned = block.shape
    nodes, cells = connectivity.shape
    slots = lax.axis_size("state")
    slabs = lax.axis_size("node")
    slot = lax.axis_index("state")
    tiles = owned // slots // LANE
    edge = tiles
    margin = HALO * LANE

    up = [(i, i + 1) for i in range(slabs - 1)]
    down = [(i + 1, i) for i in range(slabs - 1)]
    low = lax.ppermute(block[:, owned - margin :], "node", up)
    high = lax.ppermute(block[:, :margin], "node", down)

    stride = 3 * LANE // QUAD
    local = connectivity - (jnp.arange(cells, dtype=jnp.int32) * stride + ABSENT)[None, :]
    pads = ((0, 0), (0, 0), (0, LANE - nodes))
    own = jnp.stack([local.astype(jnp.float32).T, potential.T])
    own = jnp.pad(own, pads)
    send = jnp.where(slot < slots // 2, own[:, cells - 24 * QUAD :], own[:, : 24 * QUAD])
    route = [(slots * i + j, slots * (i + 1) + j) for i in range(slabs - 1) for j in range(slots // 2)]
    route += [
        (slots * (i + 1) + j, slots * i + j)
        for i in range(slabs - 1)
        for j in range(slots // 2, slots)
    ]
    other = lax.ppermute(send, ("node", "state"), route)
    spare = QUAD * UNROLL
    own = jnp.pad(own, ((0, 0), (0, spare), (0, 0)))
    other = jnp.pad(other, ((0, 0), (0, spare), (0, 0)))
    matrix = jnp.pad(cell_matrix.T, ((0, LANE - nodes), (0, LANE - nodes)))

    extended = jnp.concatenate([low, block, high], axis=1)
    width = tiles * LANE + 2 * margin
    pieces = jnp.stack([extended[:, tiles * LANE * i :][:, :width] for i in range(slots)])
    window = lax.all_to_all(pieces, "state", 0, 0).reshape(rows * slots, width)

    second, partial_sum = filtered(window, own, other, matrix, slots, tiles, edge)
    intersection = exchanged_sum(partial_sum) / (owned * slabs)
    factor, inverse = factorize(intersection)
    orthonormal = jnp.dot(inverse, second, preferred_element_type=jnp.float32).astype(jnp.bfloat16)
    orthonormal = lax.all_to_all(orthonormal, "state", 0, 1, tiled=True)
    return (orthonormal, factor)


def solution(mesh):
    return jax.shard_map(
        per_device,
        mesh=mesh,
        in_specs=(P("state", "node"), P(None, "node"), P(None, "node"), P()),
        out_specs=(P("state", "node"), P()),
        check_vma=False,
    )
```

```python
import functools

import jax
import jax.numpy as jnp
from jax import lax
from jax.experimental import pallas as pl
from jax.experimental.pallas import tpu as pltpu
from jax.sharding import Mesh
from jax.sharding import PartitionSpec as P

CENTER = 3.0
HALF_WIDTH = 3.0
LANE = 128
QUAD = 4
HALO = 6
SPARE = 5
NEAR = 24
ABSENT = 1024
CELL_TILES = ((0, 1), (0, 1, 2), (1, 2), (2, 3))
NODE_AXES = ("z", "y", "core")
STATE_AXIS = "x"
SIZES = (8, 4, 2, 4)
VMEM = pl.BlockSpec(memory_space=pltpu.VMEM)


def floor_div3(x):
    return (x + 999) // 3 - 333


def families(tiles):
    slots = lax.axis_size(STATE_AXIS)
    slot = lax.axis_index(STATE_AXIS)
    edge = tiles
    groups = slots * tiles // 2
    before = slot < slots // 2
    shift = jnp.where(before, groups - NEAR, 0)
    origin = jnp.where(before, -edge - slots * tiles, slots * tiles - edge) - tiles * slot
    return (
        (-edge - tiles * slot, 0, groups),
        (origin + 3 * shift, groups * QUAD, NEAR),
    )


def span(family, low, high):
    origin, line, groups = family
    start = jnp.maximum(-floor_div3(origin - low), 0)
    stop = jnp.minimum(floor_div3(high - origin), groups - 1)
    return line + QUAD * start, origin + 3 * start, jnp.maximum(stop - start + 1, 0)


def group_block(source, origin, acc, cells_ref, matrix_ref, segments):
    rows = lax.broadcasted_iota(jnp.int32, (LANE, LANE), 0).astype(jnp.float32)
    rows = rows.astype(jnp.bfloat16)
    one = jnp.ones((LANE, LANE), jnp.bfloat16)
    none = jnp.zeros((LANE, LANE), jnp.bfloat16)
    states, width = source.shape

    def picker(node, shift):
        row = jnp.broadcast_to(node + shift, (16, LANE)).astype(jnp.bfloat16)
        return jnp.where(rows == jnp.concatenate([row] * (LANE // 16), axis=0), one, none)

    gathered = []
    for index, (tile, lines) in enumerate(segments):
        for part, line in enumerate(lines):
            at = jnp.clip((tile + origin + 3 * part) * LANE, 0, width - 4 * LANE)
            x = source[:, pl.ds(pl.multiple_of(at, LANE), 4 * LANE)]
            pickers = []
            for cell in range(QUAD):
                node = cells_ref[0, pl.ds(line + cell, 1), :]
                pickers.append(
                    {
                        t: picker(node, 96.0 * cell - 128.0 * t + ABSENT)
                        for t in CELL_TILES[cell]
                    }
                )
            values = []
            for pair, begin in (((0, 1), 0), ((2, 3), 1)):
                weights = jnp.concatenate(
                    [
                        jnp.concatenate([pickers[c].get(t, none) for c in pair], axis=1)
                        for t in range(begin, begin + 3)
                    ],
                    axis=0,
                )
                values.append(
                    jnp.dot(
                        x[:, begin * LANE : (begin + 3) * LANE],
                        weights,
                        preferred_element_type=jnp.float32,
                    )
                )
            gathered.append((index, part, line, pickers, values))
    combined = []
    for index, part, line, pickers, values in gathered:
        half = jnp.concatenate([v.astype(jnp.bfloat16) for v in values], axis=0)
        mixed = jnp.dot(half, matrix_ref[...], preferred_element_type=jnp.float32)
        terms = []
        for pair in range(2):
            level = jnp.concatenate(
                [cells_ref[1, pl.ds(line + 2 * pair + i, 1), :] for i in range(2)], axis=1
            )
            term = mixed[states * pair : states * (pair + 1)] + level * values[pair]
            term = term.astype(jnp.bfloat16)
            terms += [term[:, :LANE], term[:, LANE:]]
        combined.append((index, part, pickers, terms))
    sums = [[None] * (3 * len(lines) + 1) for tile, lines in segments]
    for index, part, pickers, terms in combined:
        for begin, cells in ((0, (0, 1, 2)), (2, (1, 2, 3))):
            weights = jnp.concatenate(
                [
                    jnp.concatenate([pickers[c].get(t, none) for c in cells], axis=1)
                    for t in (begin, begin + 1)
                ],
                axis=0,
            )
            spread = lax.dot_general(
                jnp.concatenate([terms[c] for c in cells], axis=1),
                weights,
                (((1,), (1,)), ((), ())),
                preferred_element_type=jnp.float32,
            )
            for i in range(2):
                k = 3 * part + begin + i
                piece = spread[:, i * LANE : (i + 1) * LANE]
                total = sums[index][k]
                sums[index][k] = piece if total is None else total + piece
    for (tile, lines), pieces in zip(segments, sums):
        for k, piece in enumerate(pieces):
            at = pl.multiple_of((tile + HALO + k) * LANE, LANE)
            acc[:, pl.ds(at, LANE)] += piece


def lines_of(line, count, done, parts, blank):
    return [jnp.where(done + i < count, line + QUAD * (done + i), blank) for i in range(parts)]


def sweep(source, origin, acc, cells_ref, matrix_ref, spans, parts, blank):
    (line_a, tile_a, count_a), (line_b, tile_b, count_b) = spans
    steps_a = (count_a + parts - 1) // parts
    steps_b = (count_b + parts - 1) // parts

    def body(step, carry):
        first = step < steps_a
        done = parts * jnp.where(first, step, step - steps_a)
        line = jnp.where(first, line_a, line_b)
        tile = jnp.where(first, tile_a, tile_b) + 3 * done
        count = jnp.where(first, count_a, count_b)
        lines = lines_of(line, count, done, parts, blank)
        group_block(source, origin, acc, cells_ref, matrix_ref, [(tile, lines)])
        return carry

    lax.fori_loop(0, steps_a + steps_b, body, 0)


def interior_kernel(owned_ref, cells_ref, matrix_ref, acc_ref):
    tiles = owned_ref.shape[1] // LANE
    blank = cells_ref.shape[1] - QUAD
    acc_ref[...] = jnp.zeros_like(acc_ref)
    spans = [span(f, 0, tiles - 4) for f in families(tiles)]
    sweep(owned_ref, 0, acc_ref, cells_ref, matrix_ref, spans, 7, blank)


def rest_kernel(
    owned_ref, low_ref, high_ref, cells_ref, matrix_ref, acc_ref, second_ref, gram_ref, sum_ref, field
):
    states, owned = owned_ref.shape
    tiles = owned // LANE
    margin = HALO * LANE
    blank = cells_ref.shape[1] - QUAD
    slot = lax.axis_index(STATE_AXIS)
    slab = lax.axis_index(NODE_AXES[0])
    slabs = lax.axis_size(NODE_AXES[0])
    for axis in NODE_AXES[1:]:
        slab = slab * lax.axis_size(axis) + lax.axis_index(axis)
        slabs = slabs * lax.axis_size(axis)
    acc = sum_ref
    field[:, pl.ds(0, margin)] = low_ref[...]
    field[:, pl.ds(margin, owned)] = owned_ref[...]
    field[:, pl.ds(margin + owned, margin)] = high_ref[...]

    ends = []
    for low, high in ((-HALO, -1), (tiles - 3, tiles + 2)):
        for family in families(tiles):
            line, tile, count = span(family, low, high)
            tile = jnp.clip(tile, low, high)
            ends.append((tile, lines_of(line, count, 0, 2, blank)))
    group_block(field, HALO, acc, cells_ref, matrix_ref, ends)

    chunk = 4 * LANE
    whole = owned + 2 * margin

    def to_first(step, carry):
        here = pl.ds(pl.multiple_of(step * chunk, LANE), chunk)
        start = field[:, here].astype(jnp.float32)
        field[:, here] = ((acc[:, here] - CENTER * start) * (1.0 / HALF_WIDTH)).astype(field.dtype)
        acc[:, here] = jnp.zeros((states, chunk), jnp.float32)
        return carry

    lax.fori_loop(0, whole // chunk, to_first, 0)
    acc[:, pl.ds(whole, SPARE * LANE)] = jnp.zeros((states, SPARE * LANE), jnp.float32)

    @pl.when((slab == 0) & (slot == 0))
    def _():
        field[:, pl.ds(0, margin)] = jnp.zeros((states, margin), field.dtype)

    @pl.when((slab == slabs - 1) & (slot == lax.axis_size(STATE_AXIS) - 1))
    def _():
        field[:, pl.ds(margin + owned, margin)] = jnp.zeros((states, margin), field.dtype)

    spans = [span(f, -3, tiles - 1) for f in families(tiles)]
    sweep(field, HALO, acc, cells_ref, matrix_ref, spans, 8, blank)

    chunk = 8 * LANE

    def to_second(step, gram):
        at = pl.multiple_of(step * chunk, LANE)
        here = pl.ds(pl.multiple_of(at + margin, LANE), chunk)
        image = acc[:, here] - CENTER * field[:, here].astype(jnp.float32)
        start = owned_ref[:, pl.ds(at, chunk)].astype(jnp.float32)
        second = (image * (2.0 / HALF_WIDTH) - start).astype(second_ref.dtype)
        second_ref[:, pl.ds(at, chunk)] = second
        return gram + lax.dot_general(
            second, second, (((1,), (1,)), ((), ())), preferred_element_type=jnp.float32
        )

    gram = lax.fori_loop(0, owned // chunk, to_second, jnp.zeros((states, states), jnp.float32))
    gram_ref[...] = jnp.concatenate([gram[: states // 2], gram[states // 2 :]], axis=1)


def filtered(owned, low, high, cells, matrix):
    states, count = owned.shape
    full = count + (2 * HALO + SPARE) * LANE
    params = pltpu.CompilerParams(vmem_limit_bytes=24 << 20)
    acc = pl.pallas_call(
        interior_kernel,
        out_shape=jax.ShapeDtypeStruct((states, full), jnp.float32),
        in_specs=[VMEM] * 3,
        out_specs=VMEM,
        compiler_params=params,
        cost_estimate=pl.CostEstimate(
            flops=20_000_000_000, bytes_accessed=20_000_000, transcendentals=0
        ),
        name="interior",
    )(owned, cells, matrix)
    second, gram, unused = pl.pallas_call(
        rest_kernel,
        out_shape=(
            jax.ShapeDtypeStruct((states, count), owned.dtype),
            jax.ShapeDtypeStruct((states // 2, 2 * states), jnp.float32),
            jax.ShapeDtypeStruct((states, full), jnp.float32),
        ),
        in_specs=[VMEM] * 6,
        out_specs=[VMEM] * 3,
        input_output_aliases={5: 2},
        scratch_shapes=[pltpu.VMEM((states, count + 2 * HALO * LANE), owned.dtype)],
        compiler_params=params,
        name="rest",
    )(owned, low, high, cells, matrix, acc)
    return second, gram


def factor_kernel(total_nodes, parts_ref, second_ref, orthonormal_ref, factor_ref):
    states, owned = second_ref.shape
    packed = parts_ref[0]
    for i in range(1, parts_ref.shape[0]):
        packed = packed + parts_ref[i]
    packed = packed * (1.0 / total_nodes)
    matrix = jnp.concatenate([packed[:, :states], packed[:, states:]], axis=0)
    row_of = lax.broadcasted_iota(jnp.int32, (states, states), 0)
    col_of = lax.broadcasted_iota(jnp.int32, (states, states), 1)
    identity = jnp.where(row_of == col_of, 1.0, 0.0)
    both = jnp.concatenate([matrix, identity], axis=1)
    tall = 8
    bands = [both[tall * k : tall * (k + 1)] for k in range(states // tall)]
    within = lax.broadcasted_iota(jnp.int32, (tall, 2 * states), 0)
    for j in range(states):
        k, i = divmod(j, tall)
        row = bands[k][i : i + 1]
        scaled = row * (1.0 / row[:, j : j + 1])
        for b in range(k, len(bands)):
            update = bands[b][:, j : j + 1] * scaled
            if b == k:
                update = jnp.where(within > i, update, 0.0)
            bands[b] = bands[b] - update
    both = jnp.concatenate(bands, axis=0)
    left = both[:, :states]
    pivots = jnp.sum(jnp.where(row_of == col_of, left, 0.0), axis=1, keepdims=True)
    both = both * (1.0 / jnp.sqrt(pivots))
    left = jnp.where(col_of >= row_of, both[:, :states], 0.0)
    factor_ref[...] = left.T
    inverse = both[:, states:].astype(jnp.bfloat16)
    chunk = 16 * LANE

    def body(step, carry):
        here = pl.ds(pl.multiple_of(step * chunk, LANE), chunk)
        orthonormal_ref[:, here] = jnp.dot(
            inverse, second_ref[:, here], preferred_element_type=jnp.float32
        ).astype(orthonormal_ref.dtype)
        return carry

    lax.fori_loop(0, owned // chunk, body, 0)


def orthonormalized(parts, second, total_nodes):
    states = second.shape[0]
    return pl.pallas_call(
        functools.partial(factor_kernel, total_nodes),
        out_shape=(
            jax.ShapeDtypeStruct(second.shape, second.dtype),
            jax.ShapeDtypeStruct((states, states), jnp.float32),
        ),
        in_specs=[VMEM] * 2,
        out_specs=[VMEM] * 2,
        name="factor",
    )(parts, second)


def gathered_terms(x):
    x = x + lax.ppermute(x, "core", [(0, 1), (1, 0)])
    group = ("y", "x")
    size = lax.axis_size("y") * lax.axis_size("x")
    x = lax.all_to_all(jnp.broadcast_to(x[None], (size, *x.shape)), group, 0, 0).sum(0)
    copies = jnp.broadcast_to(x[None], (lax.axis_size("z"), *x.shape))
    return lax.all_to_all(copies, "z", 0, 0)


def neighbour_route(slabs, slots, up):
    pairs = [(i, i + 1) for i in range(slabs * slots - 1)]
    return pairs if up else [(j, i) for i, j in pairs]


def per_device(block, connectivity, potential, cell_matrix):
    nodes, cells = connectivity.shape
    slots = lax.axis_size(STATE_AXIS)
    slot = lax.axis_index(STATE_AXIS)
    slabs = lax.axis_size(NODE_AXES)
    everyone = (*NODE_AXES, STATE_AXIS)
    margin = HALO * LANE

    owned = lax.all_to_all(block, STATE_AXIS, 1, 0, tiled=True)

    stride = 3 * LANE // QUAD
    local = connectivity - (jnp.arange(cells, dtype=jnp.int32) * stride + ABSENT)[None, :]
    lines = jnp.stack([local.astype(jnp.float32).T, potential.T])
    lines = jnp.pad(lines, ((0, 0), (0, 0), (0, LANE - nodes)))
    near = NEAR * QUAD
    send = jnp.where(slot < slots // 2, lines[:, cells - near :], lines[:, :near])
    route = []
    for i in range(slabs - 1):
        for j in range(slots):
            lower, upper = slots * i + j, slots * (i + 1) + j
            route.append((lower, upper) if j < slots // 2 else (upper, lower))
    other = lax.ppermute(send, everyone, route)
    blank = jnp.zeros((2, 2 * QUAD, LANE), jnp.float32)
    lines = jnp.concatenate([lines, other, blank], axis=1)
    matrix = jnp.pad(cell_matrix.T, ((0, LANE - nodes), (0, LANE - nodes)))
    matrix = jnp.kron(jnp.eye(2, dtype=matrix.dtype), matrix)

    low = lax.ppermute(owned[:, -margin:], everyone, neighbour_route(slabs, slots, True))
    high = lax.ppermute(owned[:, :margin], everyone, neighbour_route(slabs, slots, False))
    second, gram = filtered(owned, low, high, lines, matrix)
    parts = gathered_terms(gram)
    orthonormal, factor = orthonormalized(parts, second, block.shape[1] * slabs)
    orthonormal = lax.all_to_all(orthonormal, STATE_AXIS, 0, 1, tiled=True)
    return (orthonormal, factor)


def solution(mesh):
    fine = Mesh(mesh.devices.reshape(SIZES), (*NODE_AXES, STATE_AXIS))
    return jax.shard_map(
        per_device,
        mesh=fine,
        in_specs=(P(STATE_AXIS, NODE_AXES), P(None, NODE_AXES), P(None, NODE_AXES), P()),
        out_specs=(P(STATE_AXIS, NODE_AXES), P()),
        check_vma=False,
    )
```

```python
import functools

import jax
import jax.numpy as jnp
from jax import lax
from jax.experimental import pallas as pl
from jax.experimental.pallas import tpu as pltpu
from jax.sharding import Mesh
from jax.sharding import PartitionSpec as P

CENTER = 3.0
HALF_WIDTH = 3.0
LANE = 128
QUAD = 4
HALO = 6
SPARE = 27
NEAR = 24
ABSENT = 1024
CELL_TILES = ((0, 1), (0, 1, 2), (1, 2), (2, 3))
NODE_AXES = ("z", "y", "core")
STATE_AXIS = "x"
SIZES = (8, 4, 2, 4)
VMEM = pl.BlockSpec(memory_space=pltpu.VMEM)


def floor_div3(x):
    return (x + 999) // 3 - 333


def families(tiles):
    slots = lax.axis_size(STATE_AXIS)
    slot = lax.axis_index(STATE_AXIS)
    edge = tiles
    groups = slots * tiles // 2
    before = slot < slots // 2
    shift = jnp.where(before, groups - NEAR, 0)
    origin = jnp.where(before, -edge - slots * tiles, slots * tiles - edge) - tiles * slot
    return (
        (-edge - tiles * slot, 0, groups),
        (origin + 3 * shift, groups * QUAD, NEAR),
    )


def span(family, low, high):
    origin, line, groups = family
    start = jnp.maximum(-floor_div3(origin - low), 0)
    stop = jnp.minimum(floor_div3(high - origin), groups - 1)
    return line + QUAD * start, origin + 3 * start, jnp.maximum(stop - start + 1, 0)


def group_block(source, origin, acc, cells_ref, columns_ref, matrix_ref, segments):
    def counted(axis):
        index = lax.broadcasted_iota(jnp.int32, (LANE, LANE), axis)
        return index.astype(jnp.float32).astype(jnp.bfloat16)

    down, along = counted(0), counted(1)
    one = jnp.ones((LANE, LANE), jnp.bfloat16)
    none = jnp.zeros((LANE, LANE), jnp.bfloat16)
    states, width = source.shape
    sums = [[None] * (3 * len(lines) + 1) for tile, lines in segments]
    groups = [
        (index, part, tile, line)
        for index, (tile, lines) in enumerate(segments)
        for part, line in enumerate(lines)
    ]

    def shift(cell, t):
        return 96.0 * cell - 128.0 * t + ABSENT

    def gather(index, part, tile, line):
        at = jnp.clip((tile + origin + 3 * part) * LANE, 0, width - 4 * LANE)
        x = source[:, pl.ds(pl.multiple_of(at, LANE), 4 * LANE)]
        pickers = []
        for cell in range(QUAD):
            node = cells_ref[0, pl.ds(line + cell, 1), :]
            picked = {}
            for t in CELL_TILES[cell]:
                row = jnp.broadcast_to(node + shift(cell, t), (16, LANE)).astype(jnp.bfloat16)
                row = jnp.concatenate([row] * (LANE // 16), axis=0)
                picked[t] = jnp.where(down == row, one, none)
            pickers.append(picked)
        values = []
        for pair, begin in (((0, 1), 0), ((2, 3), 1)):
            weights = jnp.concatenate(
                [
                    jnp.concatenate([pickers[c].get(t, none) for c in pair], axis=1)
                    for t in range(begin, begin + 3)
                ],
                axis=0,
            )
            x_part = x[:, begin * LANE : (begin + 3) * LANE]
            values.append(jnp.dot(x_part, weights, preferred_element_type=jnp.float32))
        return values

    def mix(values, index, part, tile, line):
        half = jnp.concatenate([v.astype(jnp.bfloat16) for v in values], axis=0)
        mixed = jnp.dot(half, matrix_ref[...], preferred_element_type=jnp.float32)
        terms = []
        for pair in range(2):
            level = jnp.concatenate(
                [cells_ref[1, pl.ds(line + 2 * pair + i, 1), :] for i in range(2)], axis=1
            )
            term = mixed[states * pair : states * (pair + 1)] + level * values[pair]
            term = term.astype(jnp.bfloat16)
            terms += [term[:, :LANE], term[:, LANE:]]
        return terms

    def scatter(terms, index, part, tile, line):
        begin = pl.multiple_of(line // LANE * LANE, LANE)
        columns = pltpu.roll(columns_ref[:, pl.ds(begin, LANE)], LANE - (line - begin), 1)
        placers = []
        for cell in range(QUAD):
            node = jnp.broadcast_to(columns[:, cell : cell + 1], (LANE, LANE))
            placers.append(
                {
                    t: jnp.where(along == (node + shift(cell, t)).astype(jnp.bfloat16), one, none)
                    for t in CELL_TILES[cell]
                }
            )
        for begin, cells in ((0, (0, 1, 2)), (2, (1, 2, 3))):
            weights = jnp.concatenate(
                [
                    jnp.concatenate([placers[c].get(t, none) for t in (begin, begin + 1)], axis=1)
                    for c in cells
                ],
                axis=0,
            )
            spread = jnp.dot(
                jnp.concatenate([terms[c] for c in cells], axis=1),
                weights,
                preferred_element_type=jnp.float32,
            )
            for i in range(2):
                k = 3 * part + begin + i
                piece = spread[:, i * LANE : (i + 1) * LANE]
                total = sums[index][k]
                sums[index][k] = piece if total is None else total + piece
        lines = segments[index][1]
        for k in range(3 * part, 3 * part + (4 if part == len(lines) - 1 else 3)):
            at = pl.multiple_of((tile + HALO + k) * LANE, LANE)
            acc[:, pl.ds(at, LANE)] += sums[index][k]

    values, terms = {}, {}
    for step in range(len(groups) + 2):
        if step < len(groups):
            values[step] = gather(*groups[step])
        if 0 <= step - 1 < len(groups):
            terms[step - 1] = mix(values.pop(step - 1), *groups[step - 1])
        if 0 <= step - 2:
            scatter(terms.pop(step - 2), *groups[step - 2])


def lines_of(line, count, done, parts, blank):
    return [jnp.where(done + i < count, line + QUAD * (done + i), blank) for i in range(parts)]


def sweep(source, origin, acc, cells_ref, columns_ref, matrix_ref, spans, parts, blank):
    (line_a, tile_a, count_a), (line_b, tile_b, count_b) = spans
    steps_a = (count_a + parts - 1) // parts
    steps_b = (count_b + parts - 1) // parts

    def body(step, carry):
        first = step < steps_a
        done = parts * jnp.where(first, step, step - steps_a)
        line = jnp.where(first, line_a, line_b)
        tile = jnp.where(first, tile_a, tile_b) + 3 * done
        count = jnp.where(first, count_a, count_b)
        lines = lines_of(line, count, done, parts, blank)
        group_block(source, origin, acc, cells_ref, columns_ref, matrix_ref, [(tile, lines)])
        return carry

    lax.fori_loop(0, steps_a + steps_b, body, 0)


def interior_kernel(owned_ref, cells_ref, columns_ref, matrix_ref, acc_ref):
    tiles = owned_ref.shape[1] // LANE
    blank = cells_ref.shape[1] - QUAD
    whole = owned_ref.shape[1] + 2 * HALO * LANE
    acc_ref[:, pl.ds(0, whole)] = jnp.zeros((acc_ref.shape[0], whole), jnp.float32)
    spans = [span(f, 0, tiles - 4) for f in families(tiles)]
    sweep(owned_ref, 0, acc_ref, cells_ref, columns_ref, matrix_ref, spans, 7, blank)


def rest_kernel(
    owned_ref,
    low_ref,
    high_ref,
    cells_ref,
    columns_ref,
    matrix_ref,
    acc_ref,
    second_ref,
    gram_ref,
    sum_ref,
    field,
):
    states, owned = owned_ref.shape
    tiles = owned // LANE
    margin = HALO * LANE
    blank = cells_ref.shape[1] - QUAD
    slot = lax.axis_index(STATE_AXIS)
    slab = lax.axis_index(NODE_AXES[0])
    slabs = lax.axis_size(NODE_AXES[0])
    for axis in NODE_AXES[1:]:
        slab = slab * lax.axis_size(axis) + lax.axis_index(axis)
        slabs = slabs * lax.axis_size(axis)
    acc = sum_ref
    field[:, pl.ds(0, margin)] = low_ref[...]
    field[:, pl.ds(margin, owned)] = owned_ref[...]
    field[:, pl.ds(margin + owned, margin)] = high_ref[...]

    ends = []
    for low, high in ((-HALO, -1), (tiles - 3, tiles + 2)):
        for family in families(tiles):
            line, tile, count = span(family, low, high)
            tile = jnp.clip(tile, low, high)
            ends.append((tile, lines_of(line, count, 0, 2, blank)))
    group_block(field, HALO, acc, cells_ref, columns_ref, matrix_ref, ends)

    chunk = 4 * LANE
    whole = owned + 2 * margin

    def to_first(step, carry):
        here = pl.ds(pl.multiple_of(step * chunk, LANE), chunk)
        start = field[:, here].astype(jnp.float32)
        field[:, here] = ((acc[:, here] - CENTER * start) * (1.0 / HALF_WIDTH)).astype(field.dtype)
        acc[:, here] = jnp.zeros((states, chunk), jnp.float32)
        return carry

    lax.fori_loop(0, whole // chunk, to_first, 0)

    @pl.when((slab == 0) & (slot == 0))
    def _():
        field[:, pl.ds(0, margin)] = jnp.zeros((states, margin), field.dtype)

    @pl.when((slab == slabs - 1) & (slot == lax.axis_size(STATE_AXIS) - 1))
    def _():
        field[:, pl.ds(margin + owned, margin)] = jnp.zeros((states, margin), field.dtype)

    spans = [span(f, -3, tiles - 1) for f in families(tiles)]
    sweep(field, HALO, acc, cells_ref, columns_ref, matrix_ref, spans, 11, blank)

    chunk = 8 * LANE

    def to_second(step, gram):
        at = pl.multiple_of(step * chunk, LANE)
        here = pl.ds(pl.multiple_of(at + margin, LANE), chunk)
        image = acc[:, here] - CENTER * field[:, here].astype(jnp.float32)
        start = owned_ref[:, pl.ds(at, chunk)].astype(jnp.float32)
        second = (image * (2.0 / HALF_WIDTH) - start).astype(second_ref.dtype)
        second_ref[:, pl.ds(at, chunk)] = second
        return gram + lax.dot_general(
            second, second, (((1,), (1,)), ((), ())), preferred_element_type=jnp.float32
        )

    gram = lax.fori_loop(0, owned // chunk, to_second, jnp.zeros((states, states), jnp.float32))
    gram_ref[...] = jnp.concatenate([gram[: states // 2], gram[states // 2 :]], axis=1)


def filtered(owned, low, high, cells, columns, matrix):
    states, count = owned.shape
    full = count + (2 * HALO + SPARE) * LANE
    params = pltpu.CompilerParams(vmem_limit_bytes=24 << 20)
    acc = pl.pallas_call(
        interior_kernel,
        out_shape=jax.ShapeDtypeStruct((states, full), jnp.float32),
        in_specs=[VMEM] * 4,
        out_specs=VMEM,
        compiler_params=params,
        cost_estimate=pl.CostEstimate(
            flops=20_000_000_000, bytes_accessed=20_000_000, transcendentals=0
        ),
        name="interior",
    )(owned, cells, columns, matrix)
    second, gram, unused = pl.pallas_call(
        rest_kernel,
        out_shape=(
            jax.ShapeDtypeStruct((states, count), owned.dtype),
            jax.ShapeDtypeStruct((states // 2, 2 * states), jnp.float32),
            jax.ShapeDtypeStruct((states, full), jnp.float32),
        ),
        in_specs=[VMEM] * 7,
        out_specs=[VMEM] * 3,
        input_output_aliases={6: 2},
        scratch_shapes=[pltpu.VMEM((states, count + 2 * HALO * LANE), owned.dtype)],
        compiler_params=params,
        name="rest",
    )(owned, low, high, cells, columns, matrix, acc)
    return second, gram


def factor_kernel(total_nodes, parts_ref, second_ref, orthonormal_ref, factor_ref):
    states, owned = second_ref.shape
    packed = parts_ref[0]
    for i in range(1, parts_ref.shape[0]):
        packed = packed + parts_ref[i]
    packed = packed * (1.0 / total_nodes)
    matrix = jnp.concatenate([packed[:, :states], packed[:, states:]], axis=0)
    row_of = lax.broadcasted_iota(jnp.int32, (states, states), 0)
    col_of = lax.broadcasted_iota(jnp.int32, (states, states), 1)
    identity = jnp.where(row_of == col_of, 1.0, 0.0)
    both = jnp.concatenate([matrix, identity], axis=1)
    tall = 8
    shape = (tall, 2 * states)
    bands = [both[tall * k : tall * (k + 1)] for k in range(states // tall)]
    within = lax.broadcasted_iota(jnp.int32, shape, 0)
    for k in range(len(bands)):
        later = bands[k + 1 :]
        rows = [jnp.broadcast_to(bands[k][i : i + 1], shape) for i in range(tall)]

        def replicated(values, i):
            return jnp.broadcast_to(values[:, tall * k + i : tall * k + i + 1], shape)

        pivot = {(i, l): replicated(rows[i], l) for i in range(tall) for l in range(i, tall)}
        columns = [[replicated(band, i) for band in later] for i in range(tall)]
        done = jnp.zeros(shape, jnp.float32)
        for i in range(tall):
            inverse = 1.0 / pivot[i, i]
            scaled = rows[i] * inverse
            done = jnp.where(within == i, rows[i] * lax.rsqrt(pivot[i, i]), done)
            later = [band - c * scaled for band, c in zip(later, columns[i])]
            for m in range(i + 1, tall):
                ratio = pivot[i, m] * inverse
                rows[m] = rows[m] - pivot[i, m] * scaled
                for l in range(m, tall):
                    pivot[m, l] = pivot[m, l] - ratio * pivot[i, l]
                columns[m] = [c - d * ratio for c, d in zip(columns[m], columns[i])]
        bands[k:] = [done, *later]
    both = jnp.concatenate(bands, axis=0)
    left = jnp.where(col_of >= row_of, both[:, :states], 0.0)
    factor_ref[...] = left.T
    inverse = both[:, states:].astype(jnp.bfloat16)
    chunk = 16 * LANE

    def body(step, carry):
        here = pl.ds(pl.multiple_of(step * chunk, LANE), chunk)
        orthonormal_ref[:, here] = jnp.dot(
            inverse, second_ref[:, here], preferred_element_type=jnp.float32
        ).astype(orthonormal_ref.dtype)
        return carry

    lax.fori_loop(0, owned // chunk, body, 0)


def orthonormalized(parts, second, total_nodes):
    states = second.shape[0]
    return pl.pallas_call(
        functools.partial(factor_kernel, total_nodes),
        out_shape=(
            jax.ShapeDtypeStruct(second.shape, second.dtype),
            jax.ShapeDtypeStruct((states, states), jnp.float32),
        ),
        in_specs=[VMEM] * 2,
        out_specs=[VMEM] * 2,
        compiler_params=pltpu.CompilerParams(vmem_limit_bytes=8 << 20),
        name="factor",
    )(parts, second)


def split_kernel(block_ref, pieces_ref, done):
    copies = []
    for i in range(pieces_ref.shape[0]):
        width = pieces_ref.shape[2]
        part = block_ref.at[:, pl.ds(i * width, width)]
        copies.append(pltpu.make_async_copy(part, pieces_ref.at[i], done.at[i]))
        copies[-1].start()
    for copy in copies:
        copy.wait()


def join_kernel(pieces_ref, block_ref, done):
    copies = []
    for i in range(pieces_ref.shape[0]):
        width = pieces_ref.shape[2]
        part = block_ref.at[:, pl.ds(i * width, width)]
        copies.append(pltpu.make_async_copy(pieces_ref.at[i], part, done.at[i]))
        copies[-1].start()
    for copy in copies:
        copy.wait()


def quarters(block, count):
    shape = (count, block.shape[0], block.shape[1] // count)
    return pl.pallas_call(
        split_kernel,
        out_shape=jax.ShapeDtypeStruct(shape, block.dtype),
        in_specs=[pl.BlockSpec(memory_space=pltpu.HBM)],
        out_specs=pl.BlockSpec(memory_space=pltpu.HBM),
        scratch_shapes=[pltpu.SemaphoreType.DMA((count,))],
        name="quarters",
    )(block)


def joined(pieces):
    count, states, width = pieces.shape
    return pl.pallas_call(
        join_kernel,
        out_shape=jax.ShapeDtypeStruct((states, count * width), pieces.dtype),
        in_specs=[VMEM],
        out_specs=pl.BlockSpec(memory_space=pl.ANY),
        scratch_shapes=[pltpu.SemaphoreType.DMA((count,))],
        compiler_params=pltpu.CompilerParams(vmem_limit_bytes=4 << 20),
        name="joined",
    )(pieces)


def gathered_terms(x):
    x = x + lax.ppermute(x, "core", [(0, 1), (1, 0)])
    group = ("y", "x")
    size = lax.axis_size("y") * lax.axis_size("x")
    x = lax.all_to_all(jnp.broadcast_to(x[None], (size, *x.shape)), group, 0, 0).sum(0)
    copies = jnp.broadcast_to(x[None], (lax.axis_size("z"), *x.shape))
    return lax.all_to_all(copies, "z", 0, 0)


def neighbour_route(slabs, slots, up):
    pairs = [(i, i + 1) for i in range(slabs * slots - 1)]
    return pairs if up else [(j, i) for i, j in pairs]


def per_device(block, connectivity, potential, cell_matrix):
    nodes, cells = connectivity.shape
    slots = lax.axis_size(STATE_AXIS)
    slot = lax.axis_index(STATE_AXIS)
    slabs = lax.axis_size(NODE_AXES)
    everyone = (*NODE_AXES, STATE_AXIS)
    margin = HALO * LANE

    pieces, connectivity, potential = lax.optimization_barrier(
        (quarters(block, slots), connectivity, potential)
    )
    pieces = lax.all_to_all(pieces, STATE_AXIS, 0, 0)
    owned = pieces.reshape(-1, pieces.shape[2])

    stride = 3 * LANE // QUAD
    local = connectivity - (jnp.arange(cells, dtype=jnp.int32) * stride + ABSENT)[None, :]
    lines = jnp.stack([local.astype(jnp.float32).T, potential.T])
    lines = jnp.pad(lines, ((0, 0), (0, 0), (0, LANE - nodes)))
    near = NEAR * QUAD
    send = jnp.where(slot < slots // 2, lines[:, cells - near :], lines[:, :near])
    route = []
    for i in range(slabs - 1):
        for j in range(slots):
            lower, upper = slots * i + j, slots * (i + 1) + j
            route.append((lower, upper) if j < slots // 2 else (upper, lower))
    other = lax.ppermute(send, everyone, route)
    blank = jnp.zeros((2, LANE - near, LANE), jnp.float32)
    other = jnp.concatenate([other, blank], axis=1)
    lines = jnp.concatenate([lines, other], axis=1)
    columns = jnp.pad(local.astype(jnp.float32), ((0, LANE - nodes), (0, 0)))
    columns = jnp.concatenate([columns, other[0].T], axis=1)
    matrix = jnp.pad(cell_matrix.T, ((0, LANE - nodes), (0, LANE - nodes)))
    matrix = jnp.kron(jnp.eye(2, dtype=matrix.dtype), matrix)

    low = lax.ppermute(owned[:, -margin:], everyone, neighbour_route(slabs, slots, True))
    high = lax.ppermute(owned[:, :margin], everyone, neighbour_route(slabs, slots, False))
    second, gram = filtered(owned, low, high, lines, columns, matrix)
    parts = gathered_terms(gram)
    orthonormal, factor = orthonormalized(parts, second, block.shape[1] * slabs)
    pieces = orthonormal.reshape(slots, -1, orthonormal.shape[1])
    pieces = lax.all_to_all(pieces, STATE_AXIS, 0, 0)
    return (joined(pieces), factor)


def solution(mesh):
    fine = Mesh(mesh.devices.reshape(SIZES), (*NODE_AXES, STATE_AXIS))
    return jax.shard_map(
        per_device,
        mesh=fine,
        in_specs=(P(STATE_AXIS, NODE_AXES), P(None, NODE_AXES), P(None, NODE_AXES), P()),
        out_specs=(P(STATE_AXIS, NODE_AXES), P()),
        check_vma=False,
    )
```

```python
import functools

import jax
import jax.numpy as jnp
from jax import lax
from jax.experimental import pallas as pl
from jax.experimental.pallas import tpu as pltpu
from jax.sharding import Mesh
from jax.sharding import PartitionSpec as P

CENTER = 3.0
HALF_WIDTH = 3.0
LANE = 128
QUAD = 4
HALO = 6
SPARE = 2
NEAR = 24
ABSENT = 1024
CELL_TILES = ((0, 1), (0, 1, 2), (1, 2), (2, 3))
NODE_AXES = ("z", "y", "core")
STATE_AXIS = "x"
SIZES = (8, 4, 2, 4)
VMEM = pl.BlockSpec(memory_space=pltpu.VMEM)


def floor_div3(x):
    return (x + 999) // 3 - 333


def families(tiles):
    slots = lax.axis_size(STATE_AXIS)
    slot = lax.axis_index(STATE_AXIS)
    edge = tiles
    groups = slots * tiles // 2
    before = slot < slots // 2
    shift = jnp.where(before, groups - NEAR, 0)
    origin = jnp.where(before, -edge - slots * tiles, slots * tiles - edge) - tiles * slot
    return (
        (-edge - tiles * slot, 0, groups),
        (origin + 3 * shift, groups * QUAD, NEAR),
    )


def span(family, low, high):
    origin, line, groups = family
    start = jnp.maximum(-floor_div3(origin - low), 0)
    stop = jnp.minimum(floor_div3(high - origin), groups - 1)
    return line + QUAD * start, origin + 3 * start, jnp.maximum(stop - start + 1, 0)


def group_block(source, origin, acc, cells_ref, columns_ref, matrix_ref, segments):
    def counted(axis):
        index = lax.broadcasted_iota(jnp.int32, (LANE, LANE), axis)
        return index.astype(jnp.float32).astype(jnp.bfloat16)

    down, along = counted(0), counted(1)
    one = jnp.ones((LANE, LANE), jnp.bfloat16)
    none = jnp.zeros((LANE, LANE), jnp.bfloat16)
    states, width = source.shape
    sums = [[None] * (3 * len(lines) + 1) for tile, lines in segments]
    groups = [
        (index, part, tile, line)
        for index, (tile, lines) in enumerate(segments)
        for part, line in enumerate(lines)
    ]

    def shift(cell, t):
        return 96.0 * cell - 128.0 * t + ABSENT

    def gather(index, part, tile, line):
        at = jnp.clip((tile + origin + 3 * part) * LANE, 0, width - 4 * LANE)
        x = source[:, pl.ds(pl.multiple_of(at, LANE), 4 * LANE)]
        pickers = []
        for cell in range(QUAD):
            node = cells_ref[0, pl.ds(line + cell, 1), :]
            picked = {}
            for t in CELL_TILES[cell]:
                row = jnp.broadcast_to(node + shift(cell, t), (16, LANE)).astype(jnp.bfloat16)
                row = jnp.concatenate([row] * (LANE // 16), axis=0)
                picked[t] = jnp.where(down == row, one, none)
            pickers.append(picked)
        values = []
        for pair, begin in (((0, 1), 0), ((2, 3), 1)):
            weights = jnp.concatenate(
                [
                    jnp.concatenate([pickers[c].get(t, none) for c in pair], axis=1)
                    for t in range(begin, begin + 3)
                ],
                axis=0,
            )
            x_part = x[:, begin * LANE : (begin + 3) * LANE]
            values.append(jnp.dot(x_part, weights, preferred_element_type=jnp.float32))
        return values

    def mix(values, index, part, tile, line):
        half = jnp.concatenate([v.astype(jnp.bfloat16) for v in values], axis=0)
        mixed = jnp.dot(half, matrix_ref[...], preferred_element_type=jnp.float32)
        terms = []
        for pair in range(2):
            level = jnp.concatenate(
                [cells_ref[1, pl.ds(line + 2 * pair + i, 1), :] for i in range(2)], axis=1
            )
            term = mixed[states * pair : states * (pair + 1)] + level * values[pair]
            term = term.astype(jnp.bfloat16)
            terms += [term[:, :LANE], term[:, LANE:]]
        return terms

    def scatter(terms, index, part, tile, line):
        begin = pl.multiple_of(line // LANE * LANE, LANE)
        columns = pltpu.roll(columns_ref[:, pl.ds(begin, LANE)], LANE - (line - begin), 1)
        placers = []
        for cell in range(QUAD):
            node = jnp.broadcast_to(columns[:, cell : cell + 1], (LANE, LANE))
            placers.append(
                {
                    t: jnp.where(along == (node + shift(cell, t)).astype(jnp.bfloat16), one, none)
                    for t in CELL_TILES[cell]
                }
            )
        for begin, cells in ((0, (0, 1, 2)), (2, (1, 2, 3))):
            weights = jnp.concatenate(
                [
                    jnp.concatenate([placers[c].get(t, none) for t in (begin, begin + 1)], axis=1)
                    for c in cells
                ],
                axis=0,
            )
            spread = jnp.dot(
                jnp.concatenate([terms[c] for c in cells], axis=1),
                weights,
                preferred_element_type=jnp.float32,
            )
            for i in range(2):
                k = 3 * part + begin + i
                piece = spread[:, i * LANE : (i + 1) * LANE]
                total = sums[index][k]
                sums[index][k] = piece if total is None else total + piece
        lines = segments[index][1]
        for k in range(3 * part, 3 * part + (4 if part == len(lines) - 1 else 3)):
            at = pl.multiple_of((tile + HALO + k) * LANE, LANE)
            acc[:, pl.ds(at, LANE)] += sums[index][k]

    values, terms = {}, {}
    for step in range(len(groups) + 2):
        if step < len(groups):
            values[step] = gather(*groups[step])
        if 0 <= step - 1 < len(groups):
            terms[step - 1] = mix(values.pop(step - 1), *groups[step - 1])
        if 0 <= step - 2:
            scatter(terms.pop(step - 2), *groups[step - 2])


def lines_of(line, count, parts, blank):
    return [jnp.where(i < count, line + QUAD * i, blank) for i in range(parts)]


def segment(family, low, high, parts, blank):
    line, tile, count = span(family, low, high)
    return jnp.clip(tile, low, low + 3), lines_of(line, count, parts, blank)


def interior_kernel(owned_ref, cells_ref, columns_ref, matrix_ref, acc_ref):
    tiles = owned_ref.shape[1] // LANE
    blank = cells_ref.shape[1] - QUAD
    whole = owned_ref.shape[1] + 2 * HALO * LANE
    acc_ref[:, pl.ds(0, whole)] = jnp.zeros((acc_ref.shape[0], whole), jnp.float32)
    parts = (tiles - 1) // 3
    inner = [segment(f, 0, tiles - 4, parts, blank) for f in families(tiles)]
    group_block(owned_ref, 0, acc_ref, cells_ref, columns_ref, matrix_ref, inner)


def rest_kernel(
    owned_ref,
    low_ref,
    high_ref,
    cells_ref,
    columns_ref,
    matrix_ref,
    acc_ref,
    second_ref,
    gram_ref,
    sum_ref,
    field,
):
    states, owned = owned_ref.shape
    tiles = owned // LANE
    margin = HALO * LANE
    blank = cells_ref.shape[1] - QUAD
    slot = lax.axis_index(STATE_AXIS)
    slab = lax.axis_index(NODE_AXES[0])
    slabs = lax.axis_size(NODE_AXES[0])
    for axis in NODE_AXES[1:]:
        slab = slab * lax.axis_size(axis) + lax.axis_index(axis)
        slabs = slabs * lax.axis_size(axis)
    acc = sum_ref
    field[:, pl.ds(0, margin)] = low_ref[...]
    field[:, pl.ds(margin, owned)] = owned_ref[...]
    field[:, pl.ds(margin + owned, margin)] = high_ref[...]

    ends = [
        segment(family, low, low + HALO - 1, 2, blank)
        for low in (-HALO, tiles - 3)
        for family in families(tiles)
    ]
    group_block(field, HALO, acc, cells_ref, columns_ref, matrix_ref, ends)

    chunk = 4 * LANE
    whole = owned + 2 * margin

    def to_first(step, carry):
        here = pl.ds(pl.multiple_of(step * chunk, LANE), chunk)
        start = field[:, here].astype(jnp.float32)
        field[:, here] = ((acc[:, here] - CENTER * start) * (1.0 / HALF_WIDTH)).astype(field.dtype)
        acc[:, here] = jnp.zeros((states, chunk), jnp.float32)
        return carry

    lax.fori_loop(0, whole // chunk, to_first, 0)

    @pl.when((slab == 0) & (slot == 0))
    def _():
        field[:, pl.ds(0, margin)] = jnp.zeros((states, margin), field.dtype)

    @pl.when((slab == slabs - 1) & (slot == lax.axis_size(STATE_AXIS) - 1))
    def _():
        field[:, pl.ds(margin + owned, margin)] = jnp.zeros((states, margin), field.dtype)

    parts = (tiles + 2) // 3
    own, other = families(tiles)
    whole_range = [
        segment(own, -3, tiles - 1, parts + 1, blank),
        segment(other, -3, tiles - 1, parts, blank),
    ]
    group_block(field, HALO, acc, cells_ref, columns_ref, matrix_ref, whole_range)

    chunk = 8 * LANE

    def to_second(step, gram):
        at = pl.multiple_of(step * chunk, LANE)
        here = pl.ds(pl.multiple_of(at + margin, LANE), chunk)
        image = acc[:, here] - CENTER * field[:, here].astype(jnp.float32)
        start = owned_ref[:, pl.ds(at, chunk)].astype(jnp.float32)
        second = (image * (2.0 / HALF_WIDTH) - start).astype(second_ref.dtype)
        second_ref[:, pl.ds(at, chunk)] = second
        return gram + lax.dot_general(
            second, second, (((1,), (1,)), ((), ())), preferred_element_type=jnp.float32
        )

    gram = lax.fori_loop(0, owned // chunk, to_second, jnp.zeros((states, states), jnp.float32))
    gram_ref[...] = jnp.concatenate([gram[: states // 2], gram[states // 2 :]], axis=1)


def filtered(owned, low, high, cells, columns, matrix):
    states, count = owned.shape
    full = count + (2 * HALO + SPARE) * LANE
    params = pltpu.CompilerParams(vmem_limit_bytes=24 << 20)
    acc = pl.pallas_call(
        interior_kernel,
        out_shape=jax.ShapeDtypeStruct((states, full), jnp.float32),
        in_specs=[VMEM] * 4,
        out_specs=VMEM,
        compiler_params=params,
        cost_estimate=pl.CostEstimate(
            flops=20_000_000_000, bytes_accessed=20_000_000, transcendentals=0
        ),
        name="interior",
    )(owned, cells, columns, matrix)
    second, gram, unused = pl.pallas_call(
        rest_kernel,
        out_shape=(
            jax.ShapeDtypeStruct((states, count), owned.dtype),
            jax.ShapeDtypeStruct((states // 2, 2 * states), jnp.float32),
            jax.ShapeDtypeStruct((states, full), jnp.float32),
        ),
        in_specs=[VMEM] * 7,
        out_specs=[VMEM] * 3,
        input_output_aliases={6: 2},
        scratch_shapes=[pltpu.VMEM((states, count + 2 * HALO * LANE), owned.dtype)],
        compiler_params=params,
        name="rest",
    )(owned, low, high, cells, columns, matrix, acc)
    return second, gram


def factor_kernel(total_nodes, parts_ref, second_ref, orthonormal_ref, factor_ref):
    states, owned = second_ref.shape
    packed = parts_ref[0]
    for i in range(1, parts_ref.shape[0]):
        packed = packed + parts_ref[i]
    packed = packed * (1.0 / total_nodes)
    matrix = jnp.concatenate([packed[:, :states], packed[:, states:]], axis=0)
    row_of = lax.broadcasted_iota(jnp.int32, (states, states), 0)
    col_of = lax.broadcasted_iota(jnp.int32, (states, states), 1)
    identity = jnp.where(row_of == col_of, 1.0, 0.0)
    both = jnp.concatenate([matrix, identity], axis=1)
    tall = 8
    shape = (tall, 2 * states)
    bands = [both[tall * k : tall * (k + 1)] for k in range(states // tall)]
    within = lax.broadcasted_iota(jnp.int32, shape, 0)
    for k in range(len(bands)):
        later = bands[k + 1 :]
        rows = [jnp.broadcast_to(bands[k][i : i + 1], shape) for i in range(tall)]

        def replicated(values, i):
            return jnp.broadcast_to(values[:, tall * k + i : tall * k + i + 1], shape)

        pivot = {(i, l): replicated(rows[i], l) for i in range(tall) for l in range(i, tall)}
        columns = [[replicated(band, i) for band in later] for i in range(tall)]
        done = jnp.zeros(shape, jnp.float32)
        for i in range(tall):
            inverse = 1.0 / pivot[i, i]
            scaled = rows[i] * inverse
            done = jnp.where(within == i, rows[i] * lax.rsqrt(pivot[i, i]), done)
            later = [band - c * scaled for band, c in zip(later, columns[i])]
            for m in range(i + 1, tall):
                ratio = pivot[i, m] * inverse
                rows[m] = rows[m] - pivot[i, m] * scaled
                for l in range(m, tall):
                    pivot[m, l] = pivot[m, l] - ratio * pivot[i, l]
                columns[m] = [c - d * ratio for c, d in zip(columns[m], columns[i])]
        bands[k:] = [done, *later]
    both = jnp.concatenate(bands, axis=0)
    left = jnp.where(col_of >= row_of, both[:, :states], 0.0)
    factor_ref[...] = left.T
    inverse = both[:, states:].astype(jnp.bfloat16)
    chunk = 16 * LANE

    def body(step, carry):
        here = pl.ds(pl.multiple_of(step * chunk, LANE), chunk)
        orthonormal_ref[:, here] = jnp.dot(
            inverse, second_ref[:, here], preferred_element_type=jnp.float32
        ).astype(orthonormal_ref.dtype)
        return carry

    lax.fori_loop(0, owned // chunk, body, 0)


def orthonormalized(parts, second, total_nodes):
    states = second.shape[0]
    return pl.pallas_call(
        functools.partial(factor_kernel, total_nodes),
        out_shape=(
            jax.ShapeDtypeStruct(second.shape, second.dtype),
            jax.ShapeDtypeStruct((states, states), jnp.float32),
        ),
        in_specs=[VMEM] * 2,
        out_specs=[VMEM] * 2,
        compiler_params=pltpu.CompilerParams(vmem_limit_bytes=8 << 20),
        name="factor",
    )(parts, second)


def split_kernel(block_ref, pieces_ref, held, came, went):
    count, states, width = pieces_ref.shape
    tall = 8
    moves = [(i, r) for r in range(0, states, tall) for i in range(count)]

    def arriving(k):
        i, r = moves[k]
        part = block_ref.at[pl.ds(r, tall), pl.ds(i * width, width)]
        return pltpu.make_async_copy(part, held.at[k], came.at[k])

    def leaving(k):
        i, r = moves[k]
        part = pieces_ref.at[i, pl.ds(r, tall), :]
        return pltpu.make_async_copy(held.at[k], part, went.at[k])

    for k in range(len(moves)):
        arriving(k).start()
    for k in range(len(moves)):
        arriving(k).wait()
        leaving(k).start()
    for k in range(len(moves)):
        leaving(k).wait()


def join_kernel(pieces_ref, block_ref, done):
    copies = []
    for i in range(pieces_ref.shape[0]):
        width = pieces_ref.shape[2]
        part = block_ref.at[:, pl.ds(i * width, width)]
        copies.append(pltpu.make_async_copy(pieces_ref.at[i], part, done.at[i]))
        copies[-1].start()
    for copy in copies:
        copy.wait()


def quarters(block, count):
    shape = (count, block.shape[0], block.shape[1] // count)
    moves = count * block.shape[0] // 8
    return pl.pallas_call(
        split_kernel,
        out_shape=jax.ShapeDtypeStruct(shape, block.dtype),
        in_specs=[pl.BlockSpec(memory_space=pltpu.HBM)],
        out_specs=pl.BlockSpec(memory_space=pltpu.HBM),
        scratch_shapes=[
            pltpu.VMEM((moves, 8, shape[2]), block.dtype),
            pltpu.SemaphoreType.DMA((moves,)),
            pltpu.SemaphoreType.DMA((moves,)),
        ],
        name="quarters",
    )(block)


def joined(pieces):
    count, states, width = pieces.shape
    return pl.pallas_call(
        join_kernel,
        out_shape=jax.ShapeDtypeStruct((states, count * width), pieces.dtype),
        in_specs=[VMEM],
        out_specs=pl.BlockSpec(memory_space=pl.ANY),
        scratch_shapes=[pltpu.SemaphoreType.DMA((count,))],
        compiler_params=pltpu.CompilerParams(vmem_limit_bytes=4 << 20),
        name="joined",
    )(pieces)


def gathered_terms(x):
    x = x + lax.ppermute(x, "core", [(0, 1), (1, 0)])
    group = ("y", "x")
    size = lax.axis_size("y") * lax.axis_size("x")
    x = lax.all_to_all(jnp.broadcast_to(x[None], (size, *x.shape)), group, 0, 0).sum(0)
    copies = jnp.broadcast_to(x[None], (lax.axis_size("z"), *x.shape))
    return lax.all_to_all(copies, "z", 0, 0)


def neighbour_route(slabs, slots, up):
    pairs = [(i, i + 1) for i in range(slabs * slots - 1)]
    return pairs if up else [(j, i) for i, j in pairs]


def per_device(block, connectivity, potential, cell_matrix):
    nodes, cells = connectivity.shape
    slots = lax.axis_size(STATE_AXIS)
    slot = lax.axis_index(STATE_AXIS)
    slabs = lax.axis_size(NODE_AXES)
    everyone = (*NODE_AXES, STATE_AXIS)
    margin = HALO * LANE

    pieces, connectivity, potential = lax.optimization_barrier(
        (quarters(block, slots), connectivity, potential)
    )
    pieces = lax.all_to_all(pieces, STATE_AXIS, 0, 0)
    owned = pieces.reshape(-1, pieces.shape[2])

    stride = 3 * LANE // QUAD
    local = connectivity - (jnp.arange(cells, dtype=jnp.int32) * stride + ABSENT)[None, :]
    lines = jnp.stack([local.astype(jnp.float32).T, potential.T])
    lines = jnp.pad(lines, ((0, 0), (0, 0), (0, LANE - nodes)))
    near = NEAR * QUAD
    send = jnp.where(slot < slots // 2, lines[:, cells - near :], lines[:, :near])
    route = []
    for i in range(slabs - 1):
        for j in range(slots):
            lower, upper = slots * i + j, slots * (i + 1) + j
            route.append((lower, upper) if j < slots // 2 else (upper, lower))
    other = lax.ppermute(send, everyone, route)
    blank = jnp.zeros((2, LANE - near, LANE), jnp.float32)
    other = jnp.concatenate([other, blank], axis=1)
    lines = jnp.concatenate([lines, other], axis=1)
    columns = jnp.pad(local.astype(jnp.float32), ((0, LANE - nodes), (0, 0)))
    columns = jnp.concatenate([columns, other[0].T], axis=1)
    matrix = jnp.pad(cell_matrix.T, ((0, LANE - nodes), (0, LANE - nodes)))
    matrix = jnp.kron(jnp.eye(2, dtype=matrix.dtype), matrix)

    low = lax.ppermute(owned[:, -margin:], everyone, neighbour_route(slabs, slots, True))
    high = lax.ppermute(owned[:, :margin], everyone, neighbour_route(slabs, slots, False))
    second, gram = filtered(owned, low, high, lines, columns, matrix)
    parts = gathered_terms(gram)
    orthonormal, factor = orthonormalized(parts, second, block.shape[1] * slabs)
    pieces = orthonormal.reshape(slots, -1, orthonormal.shape[1])
    pieces = lax.all_to_all(pieces, STATE_AXIS, 0, 0)
    return (joined(pieces), factor)


def solution(mesh):
    fine = Mesh(mesh.devices.reshape(SIZES), (*NODE_AXES, STATE_AXIS))
    return jax.shard_map(
        per_device,
        mesh=fine,
        in_specs=(P(STATE_AXIS, NODE_AXES), P(None, NODE_AXES), P(None, NODE_AXES), P()),
        out_specs=(P(STATE_AXIS, NODE_AXES), P()),
        check_vma=False,
    )
```

```python
import functools

import jax
import jax.numpy as jnp
from jax import lax
from jax.experimental import pallas as pl
from jax.experimental.pallas import tpu as pltpu
from jax.sharding import Mesh
from jax.sharding import PartitionSpec as P

CENTER = 3.0
HALF_WIDTH = 3.0
LANE = 128
QUAD = 4
HALO = 6
SPARE = 2
NEAR = 24
ABSENT = 1024
CELL_TILES = ((0, 1), (0, 1, 2), (1, 2), (2, 3))
NODE_AXES = ("z", "y", "core")
STATE_AXIS = "x"
SIZES = (8, 4, 2, 4)
VMEM = pl.BlockSpec(memory_space=pltpu.VMEM)


def floor_div3(x):
    return (x + 999) // 3 - 333


def families(tiles):
    slots = lax.axis_size(STATE_AXIS)
    slot = lax.axis_index(STATE_AXIS)
    edge = tiles
    groups = slots * tiles // 2
    before = slot < slots // 2
    shift = jnp.where(before, groups - NEAR, 0)
    origin = jnp.where(before, -edge - slots * tiles, slots * tiles - edge) - tiles * slot
    return (
        (-edge - tiles * slot, 0, groups),
        (origin + 3 * shift, groups * QUAD, NEAR),
    )


def span(family, low, high):
    origin, line, groups = family
    start = jnp.maximum(-floor_div3(origin - low), 0)
    stop = jnp.minimum(floor_div3(high - origin), groups - 1)
    return line + QUAD * start, origin + 3 * start, jnp.maximum(stop - start + 1, 0)


def group_block(source, origin, acc, cells_ref, columns_ref, matrix_ref, segments):
    def counted(axis):
        index = lax.broadcasted_iota(jnp.int32, (LANE, LANE), axis)
        return index.astype(jnp.float32).astype(jnp.bfloat16)

    down, along = counted(0), counted(1)
    one = jnp.ones((LANE, LANE), jnp.bfloat16)
    none = jnp.zeros((LANE, LANE), jnp.bfloat16)
    states, width = source.shape
    sums = [[None] * (3 * len(lines) + 1) for tile, lines in segments]
    groups = [
        (index, part, tile, line)
        for index, (tile, lines) in enumerate(segments)
        for part, line in enumerate(lines)
    ]

    def shift(cell, t):
        return 96.0 * cell - 128.0 * t + ABSENT

    def gather(index, part, tile, line):
        at = jnp.clip((tile + origin + 3 * part) * LANE, 0, width - 4 * LANE)
        x = source[:, pl.ds(pl.multiple_of(at, LANE), 4 * LANE)]
        pickers = []
        for cell in range(QUAD):
            node = cells_ref[0, pl.ds(line + cell, 1), :]
            picked = {}
            for t in CELL_TILES[cell]:
                row = jnp.broadcast_to(node + shift(cell, t), (16, LANE)).astype(jnp.bfloat16)
                row = jnp.concatenate([row] * (LANE // 16), axis=0)
                picked[t] = jnp.where(down == row, one, none)
            pickers.append(picked)
        values = []
        for pair, begin in (((0, 1), 0), ((2, 3), 1)):
            weights = jnp.concatenate(
                [
                    jnp.concatenate([pickers[c].get(t, none) for c in pair], axis=1)
                    for t in range(begin, begin + 3)
                ],
                axis=0,
            )
            x_part = x[:, begin * LANE : (begin + 3) * LANE]
            values.append(jnp.dot(x_part, weights, preferred_element_type=jnp.float32))
        return values

    def mix(values, index, part, tile, line):
        half = jnp.concatenate([v.astype(jnp.bfloat16) for v in values], axis=0)
        mixed = jnp.dot(half, matrix_ref[...], preferred_element_type=jnp.float32)
        terms = []
        for pair in range(2):
            level = jnp.concatenate(
                [cells_ref[1, pl.ds(line + 2 * pair + i, 1), :] for i in range(2)], axis=1
            )
            term = mixed[states * pair : states * (pair + 1)] + level * values[pair]
            term = term.astype(jnp.bfloat16)
            terms += [term[:, :LANE], term[:, LANE:]]
        return terms

    def scatter(terms, index, part, tile, line):
        begin = pl.multiple_of(line // LANE * LANE, LANE)
        columns = pltpu.roll(columns_ref[:, pl.ds(begin, LANE)], LANE - (line - begin), 1)
        placers = []
        for cell in range(QUAD):
            node = jnp.broadcast_to(columns[:, cell : cell + 1], (LANE, LANE))
            placers.append(
                {
                    t: jnp.where(along == (node + shift(cell, t)).astype(jnp.bfloat16), one, none)
                    for t in CELL_TILES[cell]
                }
            )
        for begin, cells in ((0, (0, 1, 2)), (2, (1, 2, 3))):
            weights = jnp.concatenate(
                [
                    jnp.concatenate([placers[c].get(t, none) for t in (begin, begin + 1)], axis=1)
                    for c in cells
                ],
                axis=0,
            )
            spread = jnp.dot(
                jnp.concatenate([terms[c] for c in cells], axis=1),
                weights,
                preferred_element_type=jnp.float32,
            )
            for i in range(2):
                k = 3 * part + begin + i
                piece = spread[:, i * LANE : (i + 1) * LANE]
                total = sums[index][k]
                sums[index][k] = piece if total is None else total + piece
        lines = segments[index][1]
        for k in range(3 * part, 3 * part + (4 if part == len(lines) - 1 else 3)):
            at = pl.multiple_of((tile + HALO + k) * LANE, LANE)
            acc[:, pl.ds(at, LANE)] += sums[index][k]

    values, terms = {}, {}
    for step in range(len(groups) + 2):
        if step < len(groups):
            values[step] = gather(*groups[step])
        if 0 <= step - 1 < len(groups):
            terms[step - 1] = mix(values.pop(step - 1), *groups[step - 1])
        if 0 <= step - 2:
            scatter(terms.pop(step - 2), *groups[step - 2])


def lines_of(line, count, parts, blank):
    return [jnp.where(i < count, line + QUAD * i, blank) for i in range(parts)]


def segment(family, low, high, parts, blank):
    line, tile, count = span(family, low, high)
    return jnp.clip(tile, low, low + 3), lines_of(line, count, parts, blank)


def interior_kernel(ends_ref, middle_ref, cells_ref, columns_ref, matrix_ref, acc_ref, window_ref):
    margin = HALO * LANE
    inner = middle_ref.shape[1]
    whole = window_ref.shape[1]
    tiles = inner // LANE + 2 * HALO
    blank = cells_ref.shape[1] - QUAD
    window_ref[:, pl.ds(margin, margin)] = ends_ref[:, pl.ds(0, margin)]
    window_ref[:, pl.ds(2 * margin, inner)] = middle_ref[...]
    window_ref[:, pl.ds(2 * margin + inner, margin)] = ends_ref[:, pl.ds(margin, margin)]
    nothing = jnp.zeros((window_ref.shape[0], margin), window_ref.dtype)
    window_ref[:, pl.ds(0, margin)] = nothing
    window_ref[:, pl.ds(whole - margin, margin)] = nothing
    acc_ref[:, pl.ds(0, whole)] = jnp.zeros((acc_ref.shape[0], whole), jnp.float32)
    parts = (tiles - 1) // 3
    inner_range = [segment(f, 0, tiles - 4, parts, blank) for f in families(tiles)]
    group_block(window_ref, HALO, acc_ref, cells_ref, columns_ref, matrix_ref, inner_range)


def rest_kernel(
    low_ref,
    high_ref,
    cells_ref,
    columns_ref,
    matrix_ref,
    acc_ref,
    window_ref,
    second_ref,
    gram_ref,
    sum_ref,
    start_ref,
    field,
):
    states, owned = second_ref.shape
    tiles = owned // LANE
    margin = HALO * LANE
    blank = cells_ref.shape[1] - QUAD
    slot = lax.axis_index(STATE_AXIS)
    slab = lax.axis_index(NODE_AXES[0])
    slabs = lax.axis_size(NODE_AXES[0])
    for axis in NODE_AXES[1:]:
        slab = slab * lax.axis_size(axis) + lax.axis_index(axis)
        slabs = slabs * lax.axis_size(axis)
    acc = sum_ref
    start_ref[:, pl.ds(0, margin)] = low_ref[...]
    start_ref[:, pl.ds(margin + owned, margin)] = high_ref[...]

    ends = [
        segment(family, low, low + HALO - 1, 2, blank)
        for low in (-HALO, tiles - 3)
        for family in families(tiles)
    ]
    group_block(start_ref, HALO, acc, cells_ref, columns_ref, matrix_ref, ends)

    chunk = 4 * LANE
    whole = owned + 2 * margin

    def to_first(step, carry):
        here = pl.ds(pl.multiple_of(step * chunk, LANE), chunk)
        start = start_ref[:, here].astype(jnp.float32)
        field[:, here] = ((acc[:, here] - CENTER * start) * (1.0 / HALF_WIDTH)).astype(field.dtype)
        acc[:, here] = jnp.zeros((states, chunk), jnp.float32)
        return carry

    lax.fori_loop(0, whole // chunk, to_first, 0)

    @pl.when((slab == 0) & (slot == 0))
    def _():
        field[:, pl.ds(0, margin)] = jnp.zeros((states, margin), field.dtype)

    @pl.when((slab == slabs - 1) & (slot == lax.axis_size(STATE_AXIS) - 1))
    def _():
        field[:, pl.ds(margin + owned, margin)] = jnp.zeros((states, margin), field.dtype)

    parts = (tiles + 2) // 3
    own, other = families(tiles)
    whole_range = [
        segment(own, -3, tiles - 1, parts + 1, blank),
        segment(other, -3, tiles - 1, parts, blank),
    ]
    group_block(field, HALO, acc, cells_ref, columns_ref, matrix_ref, whole_range)

    chunk = 8 * LANE

    def to_second(step, gram):
        at = pl.multiple_of(step * chunk, LANE)
        here = pl.ds(pl.multiple_of(at + margin, LANE), chunk)
        image = acc[:, here] - CENTER * field[:, here].astype(jnp.float32)
        start = start_ref[:, here].astype(jnp.float32)
        second = (image * (2.0 / HALF_WIDTH) - start).astype(second_ref.dtype)
        second_ref[:, pl.ds(at, chunk)] = second
        return gram + lax.dot_general(
            second, second, (((1,), (1,)), ((), ())), preferred_element_type=jnp.float32
        )

    gram = lax.fori_loop(0, owned // chunk, to_second, jnp.zeros((states, states), jnp.float32))
    gram_ref[...] = jnp.concatenate([gram[: states // 2], gram[states // 2 :]], axis=1)


def filtered(ends, middle, low, high, cells, columns, matrix):
    states, count = ends.shape[0], ends.shape[1] + middle.shape[1]
    width = count + 2 * HALO * LANE
    total = jax.ShapeDtypeStruct((states, width + SPARE * LANE), jnp.float32)
    window = jax.ShapeDtypeStruct((states, width), ends.dtype)
    params = pltpu.CompilerParams(vmem_limit_bytes=24 << 20)
    acc, start = pl.pallas_call(
        interior_kernel,
        out_shape=(total, window),
        in_specs=[VMEM] * 5,
        out_specs=[VMEM] * 2,
        compiler_params=params,
        cost_estimate=pl.CostEstimate(
            flops=20_000_000_000, bytes_accessed=20_000_000, transcendentals=0
        ),
        name="interior",
    )(ends, middle, cells, columns, matrix)
    second, gram, *unused = pl.pallas_call(
        rest_kernel,
        out_shape=(
            jax.ShapeDtypeStruct((states, count), ends.dtype),
            jax.ShapeDtypeStruct((states // 2, 2 * states), jnp.float32),
            total,
            window,
        ),
        in_specs=[VMEM] * 7,
        out_specs=[VMEM] * 4,
        input_output_aliases={5: 2, 6: 3},
        scratch_shapes=[pltpu.VMEM((states, width), ends.dtype)],
        compiler_params=params,
        name="rest",
    )(low, high, cells, columns, matrix, acc, start)
    return second, gram


def factor_kernel(total_nodes, parts_ref, second_ref, orthonormal_ref, factor_ref):
    states, owned = second_ref.shape
    packed = parts_ref[0]
    for i in range(1, parts_ref.shape[0]):
        packed = packed + parts_ref[i]
    packed = packed * (1.0 / total_nodes)
    matrix = jnp.concatenate([packed[:, :states], packed[:, states:]], axis=0)
    row_of = lax.broadcasted_iota(jnp.int32, (states, states), 0)
    col_of = lax.broadcasted_iota(jnp.int32, (states, states), 1)
    identity = jnp.where(row_of == col_of, 1.0, 0.0)
    both = jnp.concatenate([matrix, identity], axis=1)
    tall = 8
    shape = (tall, 2 * states)
    bands = [both[tall * k : tall * (k + 1)] for k in range(states // tall)]
    within = lax.broadcasted_iota(jnp.int32, shape, 0)
    for k in range(len(bands)):
        later = bands[k + 1 :]
        rows = [jnp.broadcast_to(bands[k][i : i + 1], shape) for i in range(tall)]

        def replicated(values, i):
            return jnp.broadcast_to(values[:, tall * k + i : tall * k + i + 1], shape)

        pivot = {(i, l): replicated(rows[i], l) for i in range(tall) for l in range(i, tall)}
        columns = [[replicated(band, i) for band in later] for i in range(tall)]
        done = jnp.zeros(shape, jnp.float32)
        for i in range(tall):
            inverse = 1.0 / pivot[i, i]
            scaled = rows[i] * inverse
            done = jnp.where(within == i, rows[i] * lax.rsqrt(pivot[i, i]), done)
            later = [band - c * scaled for band, c in zip(later, columns[i])]
            for m in range(i + 1, tall):
                ratio = pivot[i, m] * inverse
                rows[m] = rows[m] - pivot[i, m] * scaled
                for l in range(m, tall):
                    pivot[m, l] = pivot[m, l] - ratio * pivot[i, l]
                columns[m] = [c - d * ratio for c, d in zip(columns[m], columns[i])]
        bands[k:] = [done, *later]
    both = jnp.concatenate(bands, axis=0)
    left = jnp.where(col_of >= row_of, both[:, :states], 0.0)
    factor_ref[...] = left.T
    inverse = both[:, states:].astype(jnp.bfloat16)
    chunk = 16 * LANE

    def body(step, carry):
        here = pl.ds(pl.multiple_of(step * chunk, LANE), chunk)
        orthonormal_ref[:, here] = jnp.dot(
            inverse, second_ref[:, here], preferred_element_type=jnp.float32
        ).astype(orthonormal_ref.dtype)
        return carry

    lax.fori_loop(0, owned // chunk, body, 0)


def orthonormalized(parts, second, total_nodes):
    states = second.shape[0]
    return pl.pallas_call(
        functools.partial(factor_kernel, total_nodes),
        out_shape=(
            jax.ShapeDtypeStruct(second.shape, second.dtype),
            jax.ShapeDtypeStruct((states, states), jnp.float32),
        ),
        in_specs=[VMEM] * 2,
        out_specs=[VMEM] * 2,
        compiler_params=pltpu.CompilerParams(vmem_limit_bytes=8 << 20),
        name="factor",
    )(parts, second)


def split_kernel(block_ref, ends_ref, middle_ref, held, came, went):
    count, states, inner = middle_ref.shape
    margin = ends_ref.shape[2] // 2
    width = inner + 2 * margin
    tall = 8
    moves = [(i, r) for r in range(0, states, tall) for i in range(count)]

    def arriving(k):
        i, r = moves[k]
        part = block_ref.at[pl.ds(r, tall), pl.ds(i * width, width)]
        return pltpu.make_async_copy(part, held.at[k], came.at[k])

    def leaving(k):
        i, r = moves[k]
        low, high = pl.ds(0, margin), pl.ds(margin, margin)
        last = pl.ds(margin + inner, margin)
        pairs = [
            (held.at[k, :, low], ends_ref.at[i, pl.ds(r, tall), low]),
            (held.at[k, :, last], ends_ref.at[i, pl.ds(r, tall), high]),
            (held.at[k, :, pl.ds(margin, inner)], middle_ref.at[i, pl.ds(r, tall), :]),
        ]
        return [
            pltpu.make_async_copy(part, target, went.at[k, j])
            for j, (part, target) in enumerate(pairs)
        ]

    for k in range(len(moves)):
        arriving(k).start()
    for k in range(len(moves)):
        arriving(k).wait()
        for copy in leaving(k):
            copy.start()
    for k in range(len(moves)):
        for copy in leaving(k):
            copy.wait()


def join_kernel(pieces_ref, block_ref, done):
    copies = []
    for i in range(pieces_ref.shape[0]):
        width = pieces_ref.shape[2]
        part = block_ref.at[:, pl.ds(i * width, width)]
        copies.append(pltpu.make_async_copy(pieces_ref.at[i], part, done.at[i]))
        copies[-1].start()
    for copy in copies:
        copy.wait()


def quarters(block, count):
    states, width = block.shape[0], block.shape[1] // count
    margin = HALO * LANE
    moves = count * states // 8
    return pl.pallas_call(
        split_kernel,
        out_shape=(
            jax.ShapeDtypeStruct((count, states, 2 * margin), block.dtype),
            jax.ShapeDtypeStruct((count, states, width - 2 * margin), block.dtype),
        ),
        in_specs=[pl.BlockSpec(memory_space=pltpu.HBM)],
        out_specs=[pl.BlockSpec(memory_space=pltpu.HBM)] * 2,
        scratch_shapes=[
            pltpu.VMEM((moves, 8, width), block.dtype),
            pltpu.SemaphoreType.DMA((moves,)),
            pltpu.SemaphoreType.DMA((moves, 3)),
        ],
        name="quarters",
    )(block)


def joined(pieces):
    count, states, width = pieces.shape
    return pl.pallas_call(
        join_kernel,
        out_shape=jax.ShapeDtypeStruct((states, count * width), pieces.dtype),
        in_specs=[VMEM],
        out_specs=pl.BlockSpec(memory_space=pl.ANY),
        scratch_shapes=[pltpu.SemaphoreType.DMA((count,))],
        compiler_params=pltpu.CompilerParams(vmem_limit_bytes=4 << 20),
        name="joined",
    )(pieces)


def gathered_terms(x):
    x = x + lax.ppermute(x, "core", [(0, 1), (1, 0)])
    group = ("y", "x")
    size = lax.axis_size("y") * lax.axis_size("x")
    x = lax.all_to_all(jnp.broadcast_to(x[None], (size, *x.shape)), group, 0, 0).sum(0)
    copies = jnp.broadcast_to(x[None], (lax.axis_size("z"), *x.shape))
    return lax.all_to_all(copies, "z", 0, 0)


def neighbour_route(slabs, slots, up):
    pairs = [(i, i + 1) for i in range(slabs * slots - 1)]
    return pairs if up else [(j, i) for i, j in pairs]


def per_device(block, connectivity, potential, cell_matrix):
    nodes, cells = connectivity.shape
    slots = lax.axis_size(STATE_AXIS)
    slot = lax.axis_index(STATE_AXIS)
    slabs = lax.axis_size(NODE_AXES)
    everyone = (*NODE_AXES, STATE_AXIS)
    margin = HALO * LANE

    ends, middle, connectivity, potential = lax.optimization_barrier(
        (*quarters(block, slots), connectivity, potential)
    )
    ends = lax.all_to_all(ends, STATE_AXIS, 0, 0).reshape(-1, ends.shape[2])
    middle = lax.all_to_all(middle, STATE_AXIS, 0, 0).reshape(-1, middle.shape[2])

    stride = 3 * LANE // QUAD
    local = connectivity - (jnp.arange(cells, dtype=jnp.int32) * stride + ABSENT)[None, :]
    lines = jnp.stack([local.astype(jnp.float32).T, potential.T])
    lines = jnp.pad(lines, ((0, 0), (0, 0), (0, LANE - nodes)))
    near = NEAR * QUAD
    send = jnp.where(slot < slots // 2, lines[:, cells - near :], lines[:, :near])
    route = []
    for i in range(slabs - 1):
        for j in range(slots):
            lower, upper = slots * i + j, slots * (i + 1) + j
            route.append((lower, upper) if j < slots // 2 else (upper, lower))
    other = lax.ppermute(send, everyone, route)
    blank = jnp.zeros((2, LANE - near, LANE), jnp.float32)
    other = jnp.concatenate([other, blank], axis=1)
    lines = jnp.concatenate([lines, other], axis=1)
    columns = jnp.pad(local.astype(jnp.float32), ((0, LANE - nodes), (0, 0)))
    columns = jnp.concatenate([columns, other[0].T], axis=1)
    matrix = jnp.pad(cell_matrix.T, ((0, LANE - nodes), (0, LANE - nodes)))
    matrix = jnp.kron(jnp.eye(2, dtype=matrix.dtype), matrix)

    low = lax.ppermute(ends[:, margin:], everyone, neighbour_route(slabs, slots, True))
    high = lax.ppermute(ends[:, :margin], everyone, neighbour_route(slabs, slots, False))
    second, gram = filtered(ends, middle, low, high, lines, columns, matrix)
    parts = gathered_terms(gram)
    orthonormal, factor = orthonormalized(parts, second, block.shape[1] * slabs)
    pieces = orthonormal.reshape(slots, -1, orthonormal.shape[1])
    pieces = lax.all_to_all(pieces, STATE_AXIS, 0, 0)
    return (joined(pieces), factor)


def solution(mesh):
    fine = Mesh(mesh.devices.reshape(SIZES), (*NODE_AXES, STATE_AXIS))
    return jax.shard_map(
        per_device,
        mesh=fine,
        in_specs=(P(STATE_AXIS, NODE_AXES), P(None, NODE_AXES), P(None, NODE_AXES), P()),
        out_specs=(P(STATE_AXIS, NODE_AXES), P()),
        check_vma=False,
    )
```

```python
import functools

import jax
import jax.numpy as jnp
from jax import lax
from jax.experimental import pallas as pl
from jax.experimental.pallas import tpu as pltpu
from jax.sharding import Mesh
from jax.sharding import PartitionSpec as P

CENTER = 3.0
HALF_WIDTH = 3.0
LANE = 128
QUAD = 4
HALO = 6
SPARE = 2
NEAR = 24
ABSENT = 1024
CELL_TILES = ((0, 1), (0, 1, 2), (1, 2), (2, 3))
NODE_AXES = ("z", "y", "core")
STATE_AXIS = "x"
SIZES = (8, 4, 2, 4)
VMEM = pl.BlockSpec(memory_space=pltpu.VMEM)


def floor_div3(x):
    return (x + 999) // 3 - 333


def families(tiles):
    slots = lax.axis_size(STATE_AXIS)
    slot = lax.axis_index(STATE_AXIS)
    edge = tiles
    groups = slots * tiles // 2
    before = slot < slots // 2
    shift = jnp.where(before, groups - NEAR, 0)
    origin = jnp.where(before, -edge - slots * tiles, slots * tiles - edge) - tiles * slot
    return (
        (-edge - tiles * slot, 0, groups),
        (origin + 3 * shift, groups * QUAD, NEAR),
    )


def span(family, low, high):
    origin, line, groups = family
    start = jnp.maximum(-floor_div3(origin - low), 0)
    stop = jnp.minimum(floor_div3(high - origin), groups - 1)
    return line + QUAD * start, origin + 3 * start, jnp.maximum(stop - start + 1, 0)


def group_block(source, origin, acc, cells_ref, columns_ref, matrix_ref, segments):
    def counted(axis):
        index = lax.broadcasted_iota(jnp.int32, (LANE, LANE), axis)
        return index.astype(jnp.float32).astype(jnp.bfloat16)

    down, along = counted(0), counted(1)
    one = jnp.ones((LANE, LANE), jnp.bfloat16)
    none = jnp.zeros((LANE, LANE), jnp.bfloat16)
    states, width = source.shape
    sums = [[None] * (3 * len(lines) + 1) for tile, lines in segments]
    groups = [
        (index, part, tile, line)
        for index, (tile, lines) in enumerate(segments)
        for part, line in enumerate(lines)
    ]

    def shift(cell, t):
        return 96.0 * cell - 128.0 * t + ABSENT

    def gather(index, part, tile, line):
        at = jnp.clip((tile + origin + 3 * part) * LANE, 0, width - 4 * LANE)
        x = source[:, pl.ds(pl.multiple_of(at, LANE), 4 * LANE)]
        pickers = []
        for cell in range(QUAD):
            node = cells_ref[0, pl.ds(line + cell, 1), :]
            picked = {}
            for t in CELL_TILES[cell]:
                row = jnp.broadcast_to(node + shift(cell, t), (16, LANE)).astype(jnp.bfloat16)
                row = jnp.concatenate([row] * (LANE // 16), axis=0)
                picked[t] = jnp.where(down == row, one, none)
            pickers.append(picked)
        values = []
        for pair, begin in (((0, 1), 0), ((2, 3), 1)):
            weights = jnp.concatenate(
                [
                    jnp.concatenate([pickers[c].get(t, none) for c in pair], axis=1)
                    for t in range(begin, begin + 3)
                ],
                axis=0,
            )
            x_part = x[:, begin * LANE : (begin + 3) * LANE]
            values.append(jnp.dot(x_part, weights, preferred_element_type=jnp.float32))
        return values

    def mix(values, index, part, tile, line):
        half = jnp.concatenate([v.astype(jnp.bfloat16) for v in values], axis=0)
        mixed = jnp.dot(half, matrix_ref[...], preferred_element_type=jnp.float32)
        terms = []
        for pair in range(2):
            level = jnp.concatenate(
                [cells_ref[1, pl.ds(line + 2 * pair + i, 1), :] for i in range(2)], axis=1
            )
            term = mixed[states * pair : states * (pair + 1)] + level * values[pair]
            term = term.astype(jnp.bfloat16)
            terms += [term[:, :LANE], term[:, LANE:]]
        return terms

    def scatter(terms, index, part, tile, line):
        begin = pl.multiple_of(line // LANE * LANE, LANE)
        columns = pltpu.roll(columns_ref[:, pl.ds(begin, LANE)], LANE - (line - begin), 1)
        placers = []
        for cell in range(QUAD):
            node = jnp.broadcast_to(columns[:, cell : cell + 1], (LANE, LANE))
            placers.append(
                {
                    t: jnp.where(along == (node + shift(cell, t)).astype(jnp.bfloat16), one, none)
                    for t in CELL_TILES[cell]
                }
            )
        for begin, cells in ((0, (0, 1, 2)), (2, (1, 2, 3))):
            weights = jnp.concatenate(
                [
                    jnp.concatenate([placers[c].get(t, none) for t in (begin, begin + 1)], axis=1)
                    for c in cells
                ],
                axis=0,
            )
            spread = jnp.dot(
                jnp.concatenate([terms[c] for c in cells], axis=1),
                weights,
                preferred_element_type=jnp.float32,
            )
            for i in range(2):
                k = 3 * part + begin + i
                piece = spread[:, i * LANE : (i + 1) * LANE]
                total = sums[index][k]
                sums[index][k] = piece if total is None else total + piece
        lines = segments[index][1]
        for k in range(3 * part, 3 * part + (4 if part == len(lines) - 1 else 3)):
            at = pl.multiple_of((tile + HALO + k) * LANE, LANE)
            acc[:, pl.ds(at, LANE)] += sums[index][k]

    values, terms = {}, {}
    for step in range(len(groups) + 2):
        if step < len(groups):
            values[step] = gather(*groups[step])
        if 0 <= step - 1 < len(groups):
            terms[step - 1] = mix(values.pop(step - 1), *groups[step - 1])
        if 0 <= step - 2:
            scatter(terms.pop(step - 2), *groups[step - 2])


def lines_of(line, count, parts, blank):
    return [jnp.where(i < count, line + QUAD * i, blank) for i in range(parts)]


def segment(family, low, high, parts, blank):
    line, tile, count = span(family, low, high)
    return jnp.clip(tile, low, low + 3), lines_of(line, count, parts, blank)


def interior_kernel(ends_ref, middle_ref, cells_ref, columns_ref, matrix_ref, acc_ref, window_ref):
    margin = HALO * LANE
    inner = middle_ref.shape[1]
    whole = window_ref.shape[1]
    tiles = inner // LANE + 2 * HALO
    blank = cells_ref.shape[1] - QUAD
    window_ref[:, pl.ds(margin, margin)] = ends_ref[:, pl.ds(0, margin)]
    window_ref[:, pl.ds(2 * margin, inner)] = middle_ref[...]
    window_ref[:, pl.ds(2 * margin + inner, margin)] = ends_ref[:, pl.ds(margin, margin)]
    nothing = jnp.zeros((window_ref.shape[0], margin), window_ref.dtype)
    window_ref[:, pl.ds(0, margin)] = nothing
    window_ref[:, pl.ds(whole - margin, margin)] = nothing
    acc_ref[:, pl.ds(0, whole)] = jnp.zeros((acc_ref.shape[0], whole), jnp.float32)
    parts = (tiles - 1) // 3
    inner_range = [segment(f, 0, tiles - 4, parts, blank) for f in families(tiles)]
    group_block(window_ref, HALO, acc_ref, cells_ref, columns_ref, matrix_ref, inner_range)


def rest_kernel(
    low_ref,
    high_ref,
    cells_ref,
    columns_ref,
    matrix_ref,
    acc_ref,
    window_ref,
    second_ref,
    gram_ref,
    sum_ref,
    start_ref,
    field,
):
    states, owned = second_ref.shape
    tiles = owned // LANE
    margin = HALO * LANE
    blank = cells_ref.shape[1] - QUAD
    slot = lax.axis_index(STATE_AXIS)
    slab = lax.axis_index(NODE_AXES[0])
    slabs = lax.axis_size(NODE_AXES[0])
    for axis in NODE_AXES[1:]:
        slab = slab * lax.axis_size(axis) + lax.axis_index(axis)
        slabs = slabs * lax.axis_size(axis)
    acc = sum_ref
    start_ref[:, pl.ds(0, margin)] = low_ref[...]
    start_ref[:, pl.ds(margin + owned, margin)] = high_ref[...]

    ends = [
        segment(family, low, low + HALO - 1, 2, blank)
        for low in (-HALO, tiles - 3)
        for family in families(tiles)
    ]
    group_block(start_ref, HALO, acc, cells_ref, columns_ref, matrix_ref, ends)

    chunk = 4 * LANE
    whole = owned + 2 * margin

    def to_first(step, carry):
        here = pl.ds(pl.multiple_of(step * chunk, LANE), chunk)
        start = start_ref[:, here].astype(jnp.float32)
        field[:, here] = ((acc[:, here] - CENTER * start) * (1.0 / HALF_WIDTH)).astype(field.dtype)
        acc[:, here] = jnp.zeros((states, chunk), jnp.float32)
        return carry

    lax.fori_loop(0, whole // chunk, to_first, 0)

    @pl.when((slab == 0) & (slot == 0))
    def _():
        field[:, pl.ds(0, margin)] = jnp.zeros((states, margin), field.dtype)

    @pl.when((slab == slabs - 1) & (slot == lax.axis_size(STATE_AXIS) - 1))
    def _():
        field[:, pl.ds(margin + owned, margin)] = jnp.zeros((states, margin), field.dtype)

    parts = (tiles + 2) // 3
    own, other = families(tiles)
    whole_range = [
        segment(own, -3, tiles - 1, parts + 1, blank),
        segment(other, -3, tiles - 1, parts, blank),
    ]
    group_block(field, HALO, acc, cells_ref, columns_ref, matrix_ref, whole_range)

    chunk = 8 * LANE

    def to_second(step, gram):
        at = pl.multiple_of(step * chunk, LANE)
        here = pl.ds(pl.multiple_of(at + margin, LANE), chunk)
        image = acc[:, here] - CENTER * field[:, here].astype(jnp.float32)
        start = start_ref[:, here].astype(jnp.float32)
        second = (image * (2.0 / HALF_WIDTH) - start).astype(second_ref.dtype)
        second_ref[:, pl.ds(at, chunk)] = second
        return gram + lax.dot_general(
            second, second, (((1,), (1,)), ((), ())), preferred_element_type=jnp.float32
        )

    gram = lax.fori_loop(0, owned // chunk, to_second, jnp.zeros((states, states), jnp.float32))
    gram_ref[...] = jnp.concatenate([gram[: states // 2], gram[states // 2 :]], axis=1)


def filtered(ends, middle, low, high, cells, columns, matrix):
    states, count = ends.shape[0], ends.shape[1] + middle.shape[1]
    width = count + 2 * HALO * LANE
    total = jax.ShapeDtypeStruct((states, width + SPARE * LANE), jnp.float32)
    window = jax.ShapeDtypeStruct((states, width), ends.dtype)
    params = pltpu.CompilerParams(vmem_limit_bytes=24 << 20)
    acc, start = pl.pallas_call(
        interior_kernel,
        out_shape=(total, window),
        in_specs=[VMEM] * 5,
        out_specs=[VMEM] * 2,
        compiler_params=params,
        cost_estimate=pl.CostEstimate(
            flops=20_000_000_000, bytes_accessed=20_000_000, transcendentals=0
        ),
        name="interior",
    )(ends, middle, cells, columns, matrix)
    second, gram, *unused = pl.pallas_call(
        rest_kernel,
        out_shape=(
            jax.ShapeDtypeStruct((states, count), ends.dtype),
            jax.ShapeDtypeStruct((states // 2, 2 * states), jnp.float32),
            total,
            window,
        ),
        in_specs=[VMEM] * 7,
        out_specs=[VMEM] * 4,
        input_output_aliases={5: 2, 6: 3},
        scratch_shapes=[pltpu.VMEM((states, width), ends.dtype)],
        compiler_params=params,
        name="rest",
    )(low, high, cells, columns, matrix, acc, start)
    return second, gram


def factor_kernel(total_nodes, parts_ref, second_ref, orthonormal_ref, factor_ref):
    states, owned = second_ref.shape
    packed = parts_ref[0]
    for i in range(1, parts_ref.shape[0]):
        packed = packed + parts_ref[i]
    packed = packed * (1.0 / total_nodes)
    matrix = jnp.concatenate([packed[:, :states], packed[:, states:]], axis=0)
    row_of = lax.broadcasted_iota(jnp.int32, (states, states), 0)
    col_of = lax.broadcasted_iota(jnp.int32, (states, states), 1)
    identity = jnp.where(row_of == col_of, 1.0, 0.0)
    both = jnp.concatenate([matrix, identity], axis=1)
    tall = 8
    shape = (tall, 2 * states)
    bands = [both[tall * k : tall * (k + 1)] for k in range(states // tall)]
    within = lax.broadcasted_iota(jnp.int32, shape, 0)
    for k in range(len(bands)):
        later = bands[k + 1 :]
        rows = [jnp.broadcast_to(bands[k][i : i + 1], shape) for i in range(tall)]

        def replicated(values, i):
            return jnp.broadcast_to(values[:, tall * k + i : tall * k + i + 1], shape)

        pivot = {(i, l): replicated(rows[i], l) for i in range(tall) for l in range(i, tall)}
        columns = [[replicated(band, i) for band in later] for i in range(tall)]
        done = jnp.zeros(shape, jnp.float32)
        for i in range(tall):
            inverse = 1.0 / pivot[i, i]
            scaled = rows[i] * inverse
            done = jnp.where(within == i, rows[i] * lax.rsqrt(pivot[i, i]), done)
            later = [band - c * scaled for band, c in zip(later, columns[i])]
            for m in range(i + 1, tall):
                ratio = pivot[i, m] * inverse
                rows[m] = rows[m] - pivot[i, m] * scaled
                for l in range(m, tall):
                    pivot[m, l] = pivot[m, l] - ratio * pivot[i, l]
                columns[m] = [c - d * ratio for c, d in zip(columns[m], columns[i])]
        bands[k:] = [done, *later]
    both = jnp.concatenate(bands, axis=0)
    left = jnp.where(col_of >= row_of, both[:, :states], 0.0)
    factor_ref[...] = left.T
    inverse = both[:, states:].astype(jnp.bfloat16)
    chunk = 16 * LANE

    def body(step, carry):
        here = pl.ds(pl.multiple_of(step * chunk, LANE), chunk)
        orthonormal_ref[:, here] = jnp.dot(
            inverse, second_ref[:, here], preferred_element_type=jnp.float32
        ).astype(orthonormal_ref.dtype)
        return carry

    lax.fori_loop(0, owned // chunk, body, 0)


def orthonormalized(parts, second, total_nodes):
    states = second.shape[0]
    return pl.pallas_call(
        functools.partial(factor_kernel, total_nodes),
        out_shape=(
            jax.ShapeDtypeStruct(second.shape, second.dtype),
            jax.ShapeDtypeStruct((states, states), jnp.float32),
        ),
        in_specs=[VMEM] * 2,
        out_specs=[VMEM] * 2,
        compiler_params=pltpu.CompilerParams(vmem_limit_bytes=8 << 20),
        name="factor",
    )(parts, second)


def cut_kernel(spans, block_ref, pieces_ref, held, came, went):
    count, states, width = pieces_ref.shape
    quarter = block_ref.shape[1] // count
    tall = 8
    arriving, leaving = [], []
    for r in range(0, states, tall):
        for i in range(count):
            k = len(leaving)
            at = 0
            for j, (begin, size) in enumerate(spans):
                part = block_ref.at[pl.ds(r, tall), pl.ds(i * quarter + begin, size)]
                place = held.at[k, :, pl.ds(at, size)]
                arriving.append(pltpu.make_async_copy(part, place, came.at[k, j]))
                at += size
            piece = pieces_ref.at[i, pl.ds(r, tall), :]
            leaving.append(pltpu.make_async_copy(held.at[k], piece, went.at[k]))
    for copy in arriving:
        copy.start()
    for k, copy in enumerate(leaving):
        for j in range(len(spans)):
            arriving[k * len(spans) + j].wait()
        copy.start()
    for copy in leaving:
        copy.wait()


def join_kernel(pieces_ref, block_ref, done):
    copies = []
    for i in range(pieces_ref.shape[0]):
        width = pieces_ref.shape[2]
        part = block_ref.at[:, pl.ds(i * width, width)]
        copies.append(pltpu.make_async_copy(pieces_ref.at[i], part, done.at[i]))
        copies[-1].start()
    for copy in copies:
        copy.wait()


def cut(block, count, spans, name):
    states, width = block.shape[0], sum(size for begin, size in spans)
    moves = count * states // 8
    return pl.pallas_call(
        functools.partial(cut_kernel, spans),
        out_shape=jax.ShapeDtypeStruct((count, states, width), block.dtype),
        in_specs=[pl.BlockSpec(memory_space=pltpu.HBM)],
        out_specs=pl.BlockSpec(memory_space=pltpu.HBM),
        scratch_shapes=[
            pltpu.VMEM((moves, 8, width), block.dtype),
            pltpu.SemaphoreType.DMA((moves, len(spans))),
            pltpu.SemaphoreType.DMA((moves,)),
        ],
        name=name,
    )(block)


def joined(pieces):
    count, states, width = pieces.shape
    return pl.pallas_call(
        join_kernel,
        out_shape=jax.ShapeDtypeStruct((states, count * width), pieces.dtype),
        in_specs=[VMEM],
        out_specs=pl.BlockSpec(memory_space=pl.ANY),
        scratch_shapes=[pltpu.SemaphoreType.DMA((count,))],
        compiler_params=pltpu.CompilerParams(vmem_limit_bytes=4 << 20),
        name="joined",
    )(pieces)


def gathered_terms(x):
    x = x + lax.ppermute(x, "core", [(0, 1), (1, 0)])
    group = ("y", "x")
    size = lax.axis_size("y") * lax.axis_size("x")
    x = lax.all_to_all(jnp.broadcast_to(x[None], (size, *x.shape)), group, 0, 0).sum(0)
    copies = jnp.broadcast_to(x[None], (lax.axis_size("z"), *x.shape))
    return lax.all_to_all(copies, "z", 0, 0)


def neighbour_route(slabs, slots, up):
    pairs = [(i, i + 1) for i in range(slabs * slots - 1)]
    return pairs if up else [(j, i) for i, j in pairs]


def per_device(block, connectivity, potential, cell_matrix):
    nodes, cells = connectivity.shape
    slots = lax.axis_size(STATE_AXIS)
    slot = lax.axis_index(STATE_AXIS)
    slabs = lax.axis_size(NODE_AXES)
    everyone = (*NODE_AXES, STATE_AXIS)
    margin = HALO * LANE

    quarter = block.shape[1] // slots
    ends = cut(block, slots, ((0, margin), (quarter - margin, margin)), "ends")
    ends, block = lax.optimization_barrier((ends, block))
    middle = cut(block, slots, ((margin, quarter - 2 * margin),), "middle")
    ends = lax.all_to_all(ends, STATE_AXIS, 0, 0).reshape(-1, ends.shape[2])
    ends, connectivity, potential = lax.optimization_barrier((ends, connectivity, potential))
    middle = lax.all_to_all(middle, STATE_AXIS, 0, 0).reshape(-1, middle.shape[2])

    stride = 3 * LANE // QUAD
    local = connectivity - (jnp.arange(cells, dtype=jnp.int32) * stride + ABSENT)[None, :]
    lines = jnp.stack([local.astype(jnp.float32).T, potential.T])
    lines = jnp.pad(lines, ((0, 0), (0, 0), (0, LANE - nodes)))
    near = NEAR * QUAD
    send = jnp.where(slot < slots // 2, lines[:, cells - near :], lines[:, :near])
    route = []
    for i in range(slabs - 1):
        for j in range(slots):
            lower, upper = slots * i + j, slots * (i + 1) + j
            route.append((lower, upper) if j < slots // 2 else (upper, lower))
    other = lax.ppermute(send, everyone, route)
    blank = jnp.zeros((2, LANE - near, LANE), jnp.float32)
    other = jnp.concatenate([other, blank], axis=1)
    lines = jnp.concatenate([lines, other], axis=1)
    columns = jnp.pad(local.astype(jnp.float32), ((0, LANE - nodes), (0, 0)))
    columns = jnp.concatenate([columns, other[0].T], axis=1)
    matrix = jnp.pad(cell_matrix.T, ((0, LANE - nodes), (0, LANE - nodes)))
    matrix = jnp.kron(jnp.eye(2, dtype=matrix.dtype), matrix)

    low = lax.ppermute(ends[:, margin:], everyone, neighbour_route(slabs, slots, True))
    high = lax.ppermute(ends[:, :margin], everyone, neighbour_route(slabs, slots, False))
    second, gram = filtered(ends, middle, low, high, lines, columns, matrix)
    parts = gathered_terms(gram)
    orthonormal, factor = orthonormalized(parts, second, block.shape[1] * slabs)
    pieces = orthonormal.reshape(slots, -1, orthonormal.shape[1])
    pieces = lax.all_to_all(pieces, STATE_AXIS, 0, 0)
    return (joined(pieces), factor)


def solution(mesh):
    fine = Mesh(mesh.devices.reshape(SIZES), (*NODE_AXES, STATE_AXIS))
    return jax.shard_map(
        per_device,
        mesh=fine,
        in_specs=(P(STATE_AXIS, NODE_AXES), P(None, NODE_AXES), P(None, NODE_AXES), P()),
        out_specs=(P(STATE_AXIS, NODE_AXES), P()),
        check_vma=False,
    )
```

```python
import functools

import jax
import jax.numpy as jnp
from jax import lax
from jax.experimental import pallas as pl
from jax.experimental.pallas import tpu as pltpu
from jax.sharding import Mesh
from jax.sharding import PartitionSpec as P

CENTER = 3.0
HALF_WIDTH = 3.0
LANE = 128
QUAD = 4
HALO = 6
SPARE = 2
NEAR = 24
ABSENT = 1024
CELL_TILES = ((0, 1), (0, 1, 2), (1, 2), (2, 3))
NODE_AXES = ("z", "y", "core")
STATE_AXIS = "x"
SIZES = (8, 4, 2, 4)
VMEM = pl.BlockSpec(memory_space=pltpu.VMEM)


def floor_div3(x):
    return (x + 999) // 3 - 333


def families(tiles):
    slots = lax.axis_size(STATE_AXIS)
    slot = lax.axis_index(STATE_AXIS)
    edge = tiles
    groups = slots * tiles // 2
    before = slot < slots // 2
    shift = jnp.where(before, groups - NEAR, 0)
    origin = jnp.where(before, -edge - slots * tiles, slots * tiles - edge) - tiles * slot
    return (
        (-edge - tiles * slot, 0, groups),
        (origin + 3 * shift, groups * QUAD, NEAR),
    )


def span(family, low, high):
    origin, line, groups = family
    start = jnp.maximum(-floor_div3(origin - low), 0)
    stop = jnp.minimum(floor_div3(high - origin), groups - 1)
    return line + QUAD * start, origin + 3 * start, jnp.maximum(stop - start + 1, 0)


def group_block(source, origin, acc, cells_ref, columns_ref, matrix_ref, segments):
    def counted(axis):
        index = lax.broadcasted_iota(jnp.int32, (LANE, LANE), axis)
        return index.astype(jnp.float32).astype(jnp.bfloat16)

    down, along = counted(0), counted(1)
    one = jnp.ones((LANE, LANE), jnp.bfloat16)
    none = jnp.zeros((LANE, LANE), jnp.bfloat16)
    states, width = source.shape
    sums = [[None] * (3 * len(lines) + 1) for tile, lines in segments]
    groups = [
        (index, part, tile, line)
        for index, (tile, lines) in enumerate(segments)
        for part, line in enumerate(lines)
    ]

    def shift(cell, t):
        return 96.0 * cell - 128.0 * t + ABSENT

    def gather(index, part, tile, line):
        at = jnp.clip((tile + origin + 3 * part) * LANE, 0, width - 4 * LANE)
        x = source[:, pl.ds(pl.multiple_of(at, LANE), 4 * LANE)]
        pickers = []
        for cell in range(QUAD):
            node = cells_ref[0, pl.ds(line + cell, 1), :]
            picked = {}
            for t in CELL_TILES[cell]:
                row = jnp.broadcast_to(node + shift(cell, t), (16, LANE)).astype(jnp.bfloat16)
                row = jnp.concatenate([row] * (LANE // 16), axis=0)
                picked[t] = jnp.where(down == row, one, none)
            pickers.append(picked)
        values = []
        for pair, begin in (((0, 1), 0), ((2, 3), 1)):
            weights = jnp.concatenate(
                [
                    jnp.concatenate([pickers[c].get(t, none) for c in pair], axis=1)
                    for t in range(begin, begin + 3)
                ],
                axis=0,
            )
            x_part = x[:, begin * LANE : (begin + 3) * LANE]
            values.append(jnp.dot(x_part, weights, preferred_element_type=jnp.float32))
        return values

    def mix(values, index, part, tile, line):
        half = jnp.concatenate([v.astype(jnp.bfloat16) for v in values], axis=0)
        mixed = jnp.dot(half, matrix_ref[...], preferred_element_type=jnp.float32)
        terms = []
        for pair in range(2):
            level = jnp.concatenate(
                [cells_ref[1, pl.ds(line + 2 * pair + i, 1), :] for i in range(2)], axis=1
            )
            term = mixed[states * pair : states * (pair + 1)] + level * values[pair]
            term = term.astype(jnp.bfloat16)
            terms += [term[:, :LANE], term[:, LANE:]]
        return terms

    def scatter(terms, index, part, tile, line):
        begin = pl.multiple_of(line // LANE * LANE, LANE)
        columns = pltpu.roll(columns_ref[:, pl.ds(begin, LANE)], LANE - (line - begin), 1)
        placers = []
        for cell in range(QUAD):
            node = jnp.broadcast_to(columns[:, cell : cell + 1], (LANE, LANE))
            placers.append(
                {
                    t: jnp.where(along == (node + shift(cell, t)).astype(jnp.bfloat16), one, none)
                    for t in CELL_TILES[cell]
                }
            )
        for begin, cells in ((0, (0, 1, 2)), (2, (1, 2, 3))):
            weights = jnp.concatenate(
                [
                    jnp.concatenate([placers[c].get(t, none) for t in (begin, begin + 1)], axis=1)
                    for c in cells
                ],
                axis=0,
            )
            spread = jnp.dot(
                jnp.concatenate([terms[c] for c in cells], axis=1),
                weights,
                preferred_element_type=jnp.float32,
            )
            for i in range(2):
                k = 3 * part + begin + i
                piece = spread[:, i * LANE : (i + 1) * LANE]
                total = sums[index][k]
                sums[index][k] = piece if total is None else total + piece
        lines = segments[index][1]
        for k in range(3 * part, 3 * part + (4 if part == len(lines) - 1 else 3)):
            at = pl.multiple_of((tile + HALO + k) * LANE, LANE)
            acc[:, pl.ds(at, LANE)] += sums[index][k]

    values, terms = {}, {}
    for step in range(len(groups) + 2):
        if step < len(groups):
            values[step] = gather(*groups[step])
        if 0 <= step - 1 < len(groups):
            terms[step - 1] = mix(values.pop(step - 1), *groups[step - 1])
        if 0 <= step - 2:
            scatter(terms.pop(step - 2), *groups[step - 2])


def lines_of(line, count, parts, blank):
    return [jnp.where(i < count, line + QUAD * i, blank) for i in range(parts)]


def segment(family, low, high, parts, blank):
    line, tile, count = span(family, low, high)
    return jnp.clip(tile, low, low + 3), lines_of(line, count, parts, blank)


def interior_kernel(window_ref, cells_ref, columns_ref, matrix_ref, acc_ref):
    states, whole = window_ref.shape
    tiles = whole // LANE - 2 * HALO
    blank = cells_ref.shape[1] - QUAD
    acc_ref[:, pl.ds(0, whole)] = jnp.zeros((states, whole), jnp.float32)
    parts = (tiles - 1) // 3
    inner = [segment(f, 0, tiles - 4, parts, blank) for f in families(tiles)]
    group_block(window_ref, HALO, acc_ref, cells_ref, columns_ref, matrix_ref, inner)


def rest_kernel(
    swapped_ref,
    cells_ref,
    columns_ref,
    matrix_ref,
    acc_ref,
    window_ref,
    second_ref,
    gram_ref,
    field,
    acc,
):
    states, owned = second_ref.shape
    tiles = owned // LANE
    margin = HALO * LANE
    blank = cells_ref.shape[1] - QUAD
    slot = lax.axis_index(STATE_AXIS)
    slab = lax.axis_index(NODE_AXES[0])
    slabs = lax.axis_size(NODE_AXES[0])
    for axis in NODE_AXES[1:]:
        slab = slab * lax.axis_size(axis) + lax.axis_index(axis)
        slabs = slabs * lax.axis_size(axis)
    whole = owned + 2 * margin
    field[...] = window_ref[...]
    acc[:, pl.ds(0, whole)] = jnp.zeros((states, whole), jnp.float32)

    @pl.when(slot == 0)
    def _():
        field[:, pl.ds(0, margin)] = swapped_ref[...]

    @pl.when(slot == lax.axis_size(STATE_AXIS) - 1)
    def _():
        field[:, pl.ds(margin + owned, margin)] = swapped_ref[...]


    ends = [
        segment(family, low, low + HALO - 1, 2, blank)
        for low in (-HALO, tiles - 3)
        for family in families(tiles)
    ]
    group_block(field, HALO, acc, cells_ref, columns_ref, matrix_ref, ends)

    chunk = 4 * LANE

    def to_first(step, carry):
        here = pl.ds(pl.multiple_of(step * chunk, LANE), chunk)
        start = field[:, here].astype(jnp.float32)
        image = acc_ref[:, here] + acc[:, here] - CENTER * start
        field[:, here] = (image * (1.0 / HALF_WIDTH)).astype(field.dtype)
        acc[:, here] = jnp.zeros((states, chunk), jnp.float32)
        return carry

    lax.fori_loop(0, whole // chunk, to_first, 0)

    @pl.when((slab == 0) & (slot == 0))
    def _():
        field[:, pl.ds(0, margin)] = jnp.zeros((states, margin), field.dtype)

    @pl.when((slab == slabs - 1) & (slot == lax.axis_size(STATE_AXIS) - 1))
    def _():
        field[:, pl.ds(margin + owned, margin)] = jnp.zeros((states, margin), field.dtype)

    parts = (tiles + 2) // 3
    own, other = families(tiles)
    whole_range = [
        segment(own, -3, tiles - 1, parts + 1, blank),
        segment(other, -3, tiles - 1, parts, blank),
    ]
    group_block(field, HALO, acc, cells_ref, columns_ref, matrix_ref, whole_range)

    chunk = 16 * LANE

    def to_second(step, gram):
        at = pl.multiple_of(step * chunk, LANE)
        here = pl.ds(pl.multiple_of(at + margin, LANE), chunk)
        image = acc[:, here] - CENTER * field[:, here].astype(jnp.float32)
        start = window_ref[:, here].astype(jnp.float32)
        second = (image * (2.0 / HALF_WIDTH) - start).astype(second_ref.dtype)
        second_ref[:, pl.ds(at, chunk)] = second
        return gram + lax.dot_general(
            second, second, (((1,), (1,)), ((), ())), preferred_element_type=jnp.float32
        )

    gram = lax.fori_loop(0, owned // chunk, to_second, jnp.zeros((states, states), jnp.float32))
    gram_ref[...] = jnp.concatenate([gram[: states // 2], gram[states // 2 :]], axis=1)


def filtered(window, swapped, cells, columns, matrix):
    states, width = window.shape
    count = width - 2 * HALO * LANE
    total = jax.ShapeDtypeStruct((states, width + SPARE * LANE), jnp.float32)
    params = pltpu.CompilerParams(vmem_limit_bytes=24 << 20)
    acc = pl.pallas_call(
        interior_kernel,
        out_shape=total,
        in_specs=[VMEM] * 4,
        out_specs=VMEM,
        compiler_params=params,
        cost_estimate=pl.CostEstimate(
            flops=20_000_000_000, bytes_accessed=20_000_000, transcendentals=0
        ),
        name="interior",
    )(window, cells, columns, matrix)
    return pl.pallas_call(
        rest_kernel,
        out_shape=(
            jax.ShapeDtypeStruct((states, count), window.dtype),
            jax.ShapeDtypeStruct((states // 2, 2 * states), jnp.float32),
        ),
        in_specs=[VMEM] * 6,
        out_specs=[VMEM] * 2,
        scratch_shapes=[
            pltpu.VMEM(window.shape, window.dtype),
            pltpu.VMEM(total.shape, total.dtype),
        ],
        compiler_params=params,
        name="rest",
    )(swapped, cells, columns, matrix, acc, window)


def factor_kernel(total_nodes, parts_ref, second_ref, orthonormal_ref, factor_ref):
    states, owned = second_ref.shape
    packed = parts_ref[0]
    for i in range(1, parts_ref.shape[0]):
        packed = packed + parts_ref[i]
    packed = packed * (1.0 / total_nodes)
    matrix = jnp.concatenate([packed[:, :states], packed[:, states:]], axis=0)
    row_of = lax.broadcasted_iota(jnp.int32, (states, states), 0)
    col_of = lax.broadcasted_iota(jnp.int32, (states, states), 1)
    identity = jnp.where(row_of == col_of, 1.0, 0.0)
    both = jnp.concatenate([matrix, identity], axis=1)
    tall = 8
    shape = (tall, 2 * states)
    bands = [both[tall * k : tall * (k + 1)] for k in range(states // tall)]
    within = lax.broadcasted_iota(jnp.int32, shape, 0)
    for k in range(len(bands)):
        later = bands[k + 1 :]
        rows = [jnp.broadcast_to(bands[k][i : i + 1], shape) for i in range(tall)]

        def replicated(values, i):
            return jnp.broadcast_to(values[:, tall * k + i : tall * k + i + 1], shape)

        pivot = {(i, l): replicated(rows[i], l) for i in range(tall) for l in range(i, tall)}
        columns = [[replicated(band, i) for band in later] for i in range(tall)]
        done = jnp.zeros(shape, jnp.float32)
        for i in range(tall):
            inverse = 1.0 / pivot[i, i]
            scaled = rows[i] * inverse
            done = jnp.where(within == i, rows[i] * lax.rsqrt(pivot[i, i]), done)
            later = [band - c * scaled for band, c in zip(later, columns[i])]
            for m in range(i + 1, tall):
                ratio = pivot[i, m] * inverse
                rows[m] = rows[m] - pivot[i, m] * scaled
                for l in range(m, tall):
                    pivot[m, l] = pivot[m, l] - ratio * pivot[i, l]
                columns[m] = [c - d * ratio for c, d in zip(columns[m], columns[i])]
        bands[k:] = [done, *later]
    both = jnp.concatenate(bands, axis=0)
    left = jnp.where(col_of >= row_of, both[:, :states], 0.0)
    factor_ref[...] = left.T
    inverse = both[:, states:].astype(jnp.bfloat16)
    chunk = 16 * LANE

    def body(step, carry):
        here = pl.ds(pl.multiple_of(step * chunk, LANE), chunk)
        orthonormal_ref[:, here] = jnp.dot(
            inverse, second_ref[:, here], preferred_element_type=jnp.float32
        ).astype(orthonormal_ref.dtype)
        return carry

    lax.fori_loop(0, owned // chunk, body, 0)


def orthonormalized(parts, second, total_nodes):
    states = second.shape[0]
    return pl.pallas_call(
        functools.partial(factor_kernel, total_nodes),
        out_shape=(
            jax.ShapeDtypeStruct(second.shape, second.dtype),
            jax.ShapeDtypeStruct((states, states), jnp.float32),
        ),
        in_specs=[VMEM] * 2,
        out_specs=[VMEM] * 2,
        compiler_params=pltpu.CompilerParams(vmem_limit_bytes=8 << 20),
        name="factor",
    )(parts, second)


def window_moves(count, states, owned, margin):
    moves = []
    most = 19 * LANE
    for row in range(0, states, 8):
        for i in range(count):
            begin, place, size = owned * i - margin, 0, owned + 2 * margin
            if i == 0:
                moves.append((i, row, 0, 0, margin))
                begin, place, size = 0, margin, size - margin
            if i == count - 1:
                moves.append((i, row, owned * count - margin, owned + margin, margin))
                size -= margin
            for at in range(0, size, most):
                moves.append((i, row, begin + at, place + at, min(most, size - at)))
    return moves


def split_kernel(moves, block_ref, pieces_ref, held, came, went):
    arriving, leaving = [], []
    for k, (i, row, column, place, size) in enumerate(moves):
        rows, target = pl.ds(row, 8), pl.ds(place, size)
        source = block_ref.at[rows, pl.ds(column, size)]
        arriving.append(pltpu.make_async_copy(source, held.at[i, rows, target], came.at[k]))
        piece = pieces_ref.at[i, rows, target]
        leaving.append(pltpu.make_async_copy(held.at[i, rows, target], piece, went.at[k]))
    for copy in arriving:
        copy.start()
    for came_in, copy in zip(arriving, leaving):
        came_in.wait()
        copy.start()
    for copy in leaving:
        copy.wait()


def join_kernel(pieces_ref, block_ref, done):
    copies = []
    for i in range(pieces_ref.shape[0]):
        width = pieces_ref.shape[2]
        part = block_ref.at[:, pl.ds(i * width, width)]
        copies.append(pltpu.make_async_copy(pieces_ref.at[i], part, done.at[i]))
        copies[-1].start()
    for copy in copies:
        copy.wait()


def quarters(block, count):
    states, owned, margin = block.shape[0], block.shape[1] // count, HALO * LANE
    moves = window_moves(count, states, owned, margin)
    shape = (count, states, owned + 2 * margin)
    return pl.pallas_call(
        functools.partial(split_kernel, moves),
        out_shape=jax.ShapeDtypeStruct(shape, block.dtype),
        in_specs=[pl.BlockSpec(memory_space=pltpu.HBM)],
        out_specs=pl.BlockSpec(memory_space=pltpu.HBM),
        scratch_shapes=[
            pltpu.VMEM(shape, block.dtype),
            pltpu.SemaphoreType.DMA((len(moves),)),
            pltpu.SemaphoreType.DMA((len(moves),)),
        ],
        name="quarters",
    )(block)


def joined(pieces):
    count, states, width = pieces.shape
    return pl.pallas_call(
        join_kernel,
        out_shape=jax.ShapeDtypeStruct((states, count * width), pieces.dtype),
        in_specs=[VMEM],
        out_specs=pl.BlockSpec(memory_space=pl.ANY),
        scratch_shapes=[pltpu.SemaphoreType.DMA((count,))],
        compiler_params=pltpu.CompilerParams(vmem_limit_bytes=4 << 20),
        name="joined",
    )(pieces)


def gathered_terms(x):
    x = x + lax.ppermute(x, "core", [(0, 1), (1, 0)])
    group = ("y", "x")
    size = lax.axis_size("y") * lax.axis_size("x")
    x = lax.all_to_all(jnp.broadcast_to(x[None], (size, *x.shape)), group, 0, 0).sum(0)
    copies = jnp.broadcast_to(x[None], (lax.axis_size("z"), *x.shape))
    return lax.all_to_all(copies, "z", 0, 0)


def per_device(block, connectivity, potential, cell_matrix):
    nodes, cells = connectivity.shape
    slots = lax.axis_size(STATE_AXIS)
    slot = lax.axis_index(STATE_AXIS)
    slabs = lax.axis_size(NODE_AXES)
    everyone = (*NODE_AXES, STATE_AXIS)
    margin = HALO * LANE

    pieces, connectivity, potential = lax.optimization_barrier(
        (quarters(block, slots), connectivity, potential)
    )
    pieces = lax.all_to_all(pieces, STATE_AXIS, 0, 0)
    window = pieces.reshape(-1, pieces.shape[2])

    stride = 3 * LANE // QUAD
    local = connectivity - (jnp.arange(cells, dtype=jnp.int32) * stride + ABSENT)[None, :]
    lines = jnp.stack([local.astype(jnp.float32).T, potential.T])
    lines = jnp.pad(lines, ((0, 0), (0, 0), (0, LANE - nodes)))
    near = NEAR * QUAD
    send = jnp.where(slot < slots // 2, lines[:, cells - near :], lines[:, :near])
    route = []
    for i in range(slabs - 1):
        for j in range(slots):
            lower, upper = slots * i + j, slots * (i + 1) + j
            route.append((lower, upper) if j < slots // 2 else (upper, lower))
    other = lax.ppermute(send, everyone, route)
    blank = jnp.zeros((2, LANE - near, LANE), jnp.float32)
    other = jnp.concatenate([other, blank], axis=1)
    lines = jnp.concatenate([lines, other], axis=1)
    columns = jnp.pad(local.astype(jnp.float32), ((0, LANE - nodes), (0, 0)))
    columns = jnp.concatenate([columns, other[0].T], axis=1)
    matrix = jnp.pad(cell_matrix.T, ((0, LANE - nodes), (0, LANE - nodes)))
    matrix = jnp.kron(jnp.eye(2, dtype=matrix.dtype), matrix)

    first, last = window[:, margin : 2 * margin], window[:, -2 * margin : -margin]
    borders = [(slots * i - 1, slots * i) for i in range(1, slabs)]
    borders += [(upper, lower) for lower, upper in borders]
    swapped = lax.ppermute(jnp.where(slot == 0, first, last), everyone, borders)
    second, gram = filtered(window, swapped, lines, columns, matrix)
    parts = gathered_terms(gram)
    orthonormal, factor = orthonormalized(parts, second, block.shape[1] * slabs)
    pieces = orthonormal.reshape(slots, -1, orthonormal.shape[1])
    pieces = lax.all_to_all(pieces, STATE_AXIS, 0, 0)
    return (joined(pieces), factor)


def solution(mesh):
    fine = Mesh(mesh.devices.reshape(SIZES), (*NODE_AXES, STATE_AXIS))
    return jax.shard_map(
        per_device,
        mesh=fine,
        in_specs=(P(STATE_AXIS, NODE_AXES), P(None, NODE_AXES), P(None, NODE_AXES), P()),
        out_specs=(P(STATE_AXIS, NODE_AXES), P()),
        check_vma=False,
    )
```

```python
import functools

import jax
import jax.numpy as jnp
from jax import lax
from jax.experimental import pallas as pl
from jax.experimental.pallas import tpu as pltpu
from jax.sharding import Mesh
from jax.sharding import PartitionSpec as P

CENTER = 3.0
HALF_WIDTH = 3.0
LANE = 128
QUAD = 4
HALO = 6
SPARE = 2
NEAR = 24
ABSENT = 1024
CELL_TILES = ((0, 1), (0, 1, 2), (1, 2), (2, 3))
NODE_AXES = ("z", "y", "core")
STATE_AXIS = "x"
SIZES = (8, 4, 2, 4)
VMEM = pl.BlockSpec(memory_space=pltpu.VMEM)


def floor_div3(x):
    return (x + 999) // 3 - 333


def families(tiles):
    slots = lax.axis_size(STATE_AXIS)
    slot = lax.axis_index(STATE_AXIS)
    edge = tiles
    groups = slots * tiles // 2
    before = slot < slots // 2
    shift = jnp.where(before, groups - NEAR, 0)
    origin = jnp.where(before, -edge - slots * tiles, slots * tiles - edge) - tiles * slot
    return (
        (-edge - tiles * slot, 0, groups),
        (origin + 3 * shift, groups * QUAD, NEAR),
    )


def span(family, low, high):
    origin, line, groups = family
    start = jnp.maximum(-floor_div3(origin - low), 0)
    stop = jnp.minimum(floor_div3(high - origin), groups - 1)
    return line + QUAD * start, origin + 3 * start, jnp.maximum(stop - start + 1, 0)


def group_block(source, origin, acc, cells_ref, columns_ref, matrix_ref, segments):
    down = lax.broadcasted_iota(jnp.int32, (LANE, LANE), 0)
    down = down.astype(jnp.float32).astype(jnp.bfloat16)
    lane = lax.broadcasted_iota(jnp.int32, (16, LANE), 1)
    targets = {}
    for cell in range(QUAD):
        for t in CELL_TILES[cell]:
            row = (lane + (128 * t - 96 * cell)).astype(jnp.float32).astype(jnp.bfloat16)
            targets[cell, t] = jnp.concatenate([row] * (LANE // 16), axis=0)
    one = jnp.ones((LANE, LANE), jnp.bfloat16)
    none = jnp.zeros((LANE, LANE), jnp.bfloat16)
    states, width = source.shape
    sums = [[None] * (3 * len(lines) + 1) for tile, lines in segments]
    groups = [
        (index, part, tile, line)
        for index, (tile, lines) in enumerate(segments)
        for part, line in enumerate(lines)
    ]

    def shift(cell, t):
        return 96.0 * cell - 128.0 * t + ABSENT

    def gather(index, part, tile, line):
        at = jnp.clip((tile + origin + 3 * part) * LANE, 0, width - 4 * LANE)
        x = source[:, pl.ds(pl.multiple_of(at, LANE), 4 * LANE)]
        pickers = []
        for cell in range(QUAD):
            node = cells_ref[0, pl.ds(line + cell, 1), :]
            picked = {}
            for t in CELL_TILES[cell]:
                row = jnp.broadcast_to(node + shift(cell, t), (16, LANE)).astype(jnp.bfloat16)
                row = jnp.concatenate([row] * (LANE // 16), axis=0)
                picked[t] = jnp.where(down == row, one, none)
            pickers.append(picked)
        values = []
        for pair, begin in (((0, 1), 0), ((2, 3), 1)):
            weights = jnp.concatenate(
                [
                    jnp.concatenate([pickers[c].get(t, none) for c in pair], axis=1)
                    for t in range(begin, begin + 3)
                ],
                axis=0,
            )
            x_part = x[:, begin * LANE : (begin + 3) * LANE]
            values.append(jnp.dot(x_part, weights, preferred_element_type=jnp.float32))
        return values

    def mix(values, index, part, tile, line):
        half = jnp.concatenate([v.astype(jnp.bfloat16) for v in values], axis=0)
        mixed = jnp.dot(half, matrix_ref[...], preferred_element_type=jnp.float32)
        terms = []
        for pair in range(2):
            level = jnp.concatenate(
                [cells_ref[1, pl.ds(line + 2 * pair + i, 1), :] for i in range(2)], axis=1
            )
            term = mixed[states * pair : states * (pair + 1)] + level * values[pair]
            term = term.astype(jnp.bfloat16)
            terms += [term[:, :LANE], term[:, LANE:]]
        return terms

    def scatter(terms, index, part, tile, line):
        begin = pl.multiple_of(line // LANE * LANE, LANE)
        columns = columns_ref[:, pl.ds(begin, LANE)]
        placers = []
        for cell in range(QUAD):
            lanes = jnp.full((8, LANE), line - begin + cell, jnp.int32)
            node = jnp.concatenate(
                [
                    jnp.take_along_axis(columns[k : k + 8], lanes, axis=1)
                    for k in range(0, LANE, 8)
                ],
                axis=0,
            )
            node = (node + ABSENT).astype(jnp.bfloat16)
            placers.append(
                {t: jnp.where(node == targets[cell, t], one, none) for t in CELL_TILES[cell]}
            )
        for begin, cells in ((0, (0, 1, 2)), (2, (1, 2, 3))):
            weights = jnp.concatenate(
                [
                    jnp.concatenate([placers[c].get(t, none) for t in (begin, begin + 1)], axis=1)
                    for c in cells
                ],
                axis=0,
            )
            spread = jnp.dot(
                jnp.concatenate([terms[c] for c in cells], axis=1),
                weights,
                preferred_element_type=jnp.float32,
            )
            for i in range(2):
                k = 3 * part + begin + i
                piece = spread[:, i * LANE : (i + 1) * LANE]
                total = sums[index][k]
                sums[index][k] = piece if total is None else total + piece
        lines = segments[index][1]
        for k in range(3 * part, 3 * part + (4 if part == len(lines) - 1 else 3)):
            at = pl.multiple_of((tile + HALO + k) * LANE, LANE)
            acc[:, pl.ds(at, LANE)] += sums[index][k]

    values, terms = {}, {}
    for step in range(len(groups) + 2):
        if step < len(groups):
            values[step] = gather(*groups[step])
        if 0 <= step - 1 < len(groups):
            terms[step - 1] = mix(values.pop(step - 1), *groups[step - 1])
        if 0 <= step - 2:
            scatter(terms.pop(step - 2), *groups[step - 2])


def lines_of(line, count, parts, blank):
    return [jnp.where(i < count, line + QUAD * i, blank) for i in range(parts)]


def segment(family, low, high, parts, blank):
    line, tile, count = span(family, low, high)
    return jnp.clip(tile, low, low + 3), lines_of(line, count, parts, blank)


def interior_kernel(window_ref, cells_ref, columns_ref, matrix_ref, acc_ref):
    states, whole = window_ref.shape
    tiles = whole // LANE - 2 * HALO
    blank = cells_ref.shape[1] - QUAD
    acc_ref[:, pl.ds(0, whole)] = jnp.zeros((states, whole), jnp.float32)
    parts = (tiles - 1) // 3
    inner = [segment(f, 0, tiles - 4, parts, blank) for f in families(tiles)]
    group_block(window_ref, HALO, acc_ref, cells_ref, columns_ref, matrix_ref, inner)


def rest_kernel(
    swapped_ref,
    cells_ref,
    columns_ref,
    matrix_ref,
    acc_ref,
    window_ref,
    second_ref,
    gram_ref,
    field,
    acc,
):
    states, owned = second_ref.shape
    tiles = owned // LANE
    margin = HALO * LANE
    blank = cells_ref.shape[1] - QUAD
    slot = lax.axis_index(STATE_AXIS)
    slab = lax.axis_index(NODE_AXES[0])
    slabs = lax.axis_size(NODE_AXES[0])
    for axis in NODE_AXES[1:]:
        slab = slab * lax.axis_size(axis) + lax.axis_index(axis)
        slabs = slabs * lax.axis_size(axis)
    whole = owned + 2 * margin
    field[...] = window_ref[...]
    acc[:, pl.ds(0, whole)] = jnp.zeros((states, whole), jnp.float32)

    @pl.when(slot == 0)
    def _():
        field[:, pl.ds(0, margin)] = swapped_ref[...]

    @pl.when(slot == lax.axis_size(STATE_AXIS) - 1)
    def _():
        field[:, pl.ds(margin + owned, margin)] = swapped_ref[...]


    ends = [
        segment(family, low, low + HALO - 1, 2, blank)
        for low in (-HALO, tiles - 3)
        for family in families(tiles)
    ]
    group_block(field, HALO, acc, cells_ref, columns_ref, matrix_ref, ends)

    chunk = 4 * LANE

    def to_first(step, carry):
        here = pl.ds(pl.multiple_of(step * chunk, LANE), chunk)
        start = field[:, here].astype(jnp.float32)
        image = acc_ref[:, here] + acc[:, here] - CENTER * start
        field[:, here] = (image * (1.0 / HALF_WIDTH)).astype(field.dtype)
        acc[:, here] = jnp.zeros((states, chunk), jnp.float32)
        return carry

    lax.fori_loop(0, whole // chunk, to_first, 0)

    @pl.when((slab == 0) & (slot == 0))
    def _():
        field[:, pl.ds(0, margin)] = jnp.zeros((states, margin), field.dtype)

    @pl.when((slab == slabs - 1) & (slot == lax.axis_size(STATE_AXIS) - 1))
    def _():
        field[:, pl.ds(margin + owned, margin)] = jnp.zeros((states, margin), field.dtype)

    parts = (tiles + 2) // 3
    own, other = families(tiles)
    whole_range = [
        segment(own, -3, tiles - 1, parts + 1, blank),
        segment(other, -3, tiles - 1, parts, blank),
    ]
    group_block(field, HALO, acc, cells_ref, columns_ref, matrix_ref, whole_range)

    chunk = 16 * LANE

    def to_second(step, gram):
        at = pl.multiple_of(step * chunk, LANE)
        here = pl.ds(pl.multiple_of(at + margin, LANE), chunk)
        image = acc[:, here] - CENTER * field[:, here].astype(jnp.float32)
        start = window_ref[:, here].astype(jnp.float32)
        second = (image * (2.0 / HALF_WIDTH) - start).astype(second_ref.dtype)
        second_ref[:, pl.ds(at, chunk)] = second
        return gram + lax.dot_general(
            second, second, (((1,), (1,)), ((), ())), preferred_element_type=jnp.float32
        )

    gram = lax.fori_loop(0, owned // chunk, to_second, jnp.zeros((states, states), jnp.float32))
    gram_ref[...] = jnp.concatenate([gram[: states // 2], gram[states // 2 :]], axis=1)


def filtered(window, swapped, cells, columns, matrix):
    states, width = window.shape
    count = width - 2 * HALO * LANE
    total = jax.ShapeDtypeStruct((states, width + SPARE * LANE), jnp.float32)
    params = pltpu.CompilerParams(vmem_limit_bytes=24 << 20)
    acc = pl.pallas_call(
        interior_kernel,
        out_shape=total,
        in_specs=[VMEM] * 4,
        out_specs=VMEM,
        compiler_params=params,
        cost_estimate=pl.CostEstimate(
            flops=20_000_000_000, bytes_accessed=20_000_000, transcendentals=0
        ),
        name="interior",
    )(window, cells, columns, matrix)
    return pl.pallas_call(
        rest_kernel,
        out_shape=(
            jax.ShapeDtypeStruct((states, count), window.dtype),
            jax.ShapeDtypeStruct((states // 2, 2 * states), jnp.float32),
        ),
        in_specs=[VMEM] * 6,
        out_specs=[VMEM] * 2,
        scratch_shapes=[
            pltpu.VMEM(window.shape, window.dtype),
            pltpu.VMEM(total.shape, total.dtype),
        ],
        compiler_params=params,
        name="rest",
    )(swapped, cells, columns, matrix, acc, window)


def factor_kernel(total_nodes, parts_ref, second_ref, orthonormal_ref, factor_ref):
    states, owned = second_ref.shape
    packed = parts_ref[0]
    for i in range(1, parts_ref.shape[0]):
        packed = packed + parts_ref[i]
    packed = packed * (1.0 / total_nodes)
    matrix = jnp.concatenate([packed[:, :states], packed[:, states:]], axis=0)
    row_of = lax.broadcasted_iota(jnp.int32, (states, states), 0)
    col_of = lax.broadcasted_iota(jnp.int32, (states, states), 1)
    identity = jnp.where(row_of == col_of, 1.0, 0.0)
    both = jnp.concatenate([matrix, identity], axis=1)
    tall = 8
    shape = (tall, 2 * states)
    bands = [both[tall * k : tall * (k + 1)] for k in range(states // tall)]
    within = lax.broadcasted_iota(jnp.int32, shape, 0)
    for k in range(len(bands)):
        later = bands[k + 1 :]
        rows = [jnp.broadcast_to(bands[k][i : i + 1], shape) for i in range(tall)]

        def replicated(values, i):
            return jnp.broadcast_to(values[:, tall * k + i : tall * k + i + 1], shape)

        pivot = {(i, l): replicated(rows[i], l) for i in range(tall) for l in range(i, tall)}
        columns = [[replicated(band, i) for band in later] for i in range(tall)]
        done = jnp.zeros(shape, jnp.float32)
        for i in range(tall):
            inverse = 1.0 / pivot[i, i]
            scaled = rows[i] * inverse
            done = jnp.where(within == i, rows[i] * lax.rsqrt(pivot[i, i]), done)
            later = [band - c * scaled for band, c in zip(later, columns[i])]
            for m in range(i + 1, tall):
                ratio = pivot[i, m] * inverse
                rows[m] = rows[m] - pivot[i, m] * scaled
                for l in range(m, tall):
                    pivot[m, l] = pivot[m, l] - ratio * pivot[i, l]
                columns[m] = [c - d * ratio for c, d in zip(columns[m], columns[i])]
        bands[k:] = [done, *later]
    both = jnp.concatenate(bands, axis=0)
    left = jnp.where(col_of >= row_of, both[:, :states], 0.0)
    factor_ref[...] = left.T
    inverse = both[:, states:].astype(jnp.bfloat16)
    chunk = 16 * LANE

    def body(step, carry):
        here = pl.ds(pl.multiple_of(step * chunk, LANE), chunk)
        orthonormal_ref[:, here] = jnp.dot(
            inverse, second_ref[:, here], preferred_element_type=jnp.float32
        ).astype(orthonormal_ref.dtype)
        return carry

    lax.fori_loop(0, owned // chunk, body, 0)


def orthonormalized(parts, second, total_nodes):
    states = second.shape[0]
    return pl.pallas_call(
        functools.partial(factor_kernel, total_nodes),
        out_shape=(
            jax.ShapeDtypeStruct(second.shape, second.dtype),
            jax.ShapeDtypeStruct((states, states), jnp.float32),
        ),
        in_specs=[VMEM] * 2,
        out_specs=[VMEM] * 2,
        compiler_params=pltpu.CompilerParams(vmem_limit_bytes=8 << 20),
        name="factor",
    )(parts, second)


def split_kernel(block_ref, pieces_ref, held, came, went):
    count, states, width = pieces_ref.shape
    total = block_ref.shape[1]
    margin = HALO * LANE
    owned = total // count
    tall, wide = 8, total // 2
    arriving = [(row, at) for row in range(0, states, tall) for at in range(0, total, wide)]
    leaving = []
    for row in range(0, states, tall):
        for i in range(count):
            begin, place, size = owned * i - margin, 0, width
            if i == 0:
                leaving.append((i, row, 0, 0, margin))
                begin, place, size = 0, margin, size - margin
            if i == count - 1:
                leaving.append((i, row, total - margin, width - margin, margin))
                size -= margin
            leaving.append((i, row, begin, place, size))

    def copy_in(k):
        row, at = arriving[k]
        part = (pl.ds(row, tall), pl.ds(at, wide))
        return pltpu.make_async_copy(block_ref.at[part], held.at[part], came.at[k])

    def copy_out(k):
        i, row, column, place, size = leaving[k]
        source = held.at[pl.ds(row, tall), pl.ds(column, size)]
        target = pieces_ref.at[i, pl.ds(row, tall), pl.ds(place, size)]
        return pltpu.make_async_copy(source, target, went.at[k])

    for k in range(len(arriving)):
        copy_in(k).start()
    left = list(range(len(leaving)))
    for k, (row, at) in enumerate(arriving):
        copy_in(k).wait()
        for j in list(left):
            i, state, column, place, size = leaving[j]
            if state < row or (state == row and column + size <= at + wide):
                copy_out(j).start()
                left.remove(j)
    for k in range(len(leaving)):
        copy_out(k).wait()


def join_kernel(pieces_ref, block_ref, done):
    copies = []
    for i in range(pieces_ref.shape[0]):
        width = pieces_ref.shape[2]
        part = block_ref.at[:, pl.ds(i * width, width)]
        copies.append(pltpu.make_async_copy(pieces_ref.at[i], part, done.at[i]))
        copies[-1].start()
    for copy in copies:
        copy.wait()


def quarters(block, count):
    states, total = block.shape
    shape = (count, states, total // count + 2 * HALO * LANE)
    return pl.pallas_call(
        split_kernel,
        out_shape=jax.ShapeDtypeStruct(shape, block.dtype),
        in_specs=[pl.BlockSpec(memory_space=pltpu.HBM)],
        out_specs=pl.BlockSpec(memory_space=pltpu.HBM),
        scratch_shapes=[
            pltpu.VMEM(block.shape, block.dtype),
            pltpu.SemaphoreType.DMA((states // 4,)),
            pltpu.SemaphoreType.DMA((states // 8 * (count + 2),)),
        ],
        name="quarters",
    )(block)


def joined(pieces):
    count, states, width = pieces.shape
    return pl.pallas_call(
        join_kernel,
        out_shape=jax.ShapeDtypeStruct((states, count * width), pieces.dtype),
        in_specs=[VMEM],
        out_specs=pl.BlockSpec(memory_space=pl.ANY),
        scratch_shapes=[pltpu.SemaphoreType.DMA((count,))],
        compiler_params=pltpu.CompilerParams(vmem_limit_bytes=4 << 20),
        name="joined",
    )(pieces)


def gathered_terms(x):
    x = x + lax.ppermute(x, "core", [(0, 1), (1, 0)])
    group = ("y", "x")
    size = lax.axis_size("y") * lax.axis_size("x")
    x = lax.all_to_all(jnp.broadcast_to(x[None], (size, *x.shape)), group, 0, 0).sum(0)
    copies = jnp.broadcast_to(x[None], (lax.axis_size("z"), *x.shape))
    return lax.all_to_all(copies, "z", 0, 0)


def per_device(block, connectivity, potential, cell_matrix):
    nodes, cells = connectivity.shape
    slots = lax.axis_size(STATE_AXIS)
    slot = lax.axis_index(STATE_AXIS)
    slabs = lax.axis_size(NODE_AXES)
    everyone = (*NODE_AXES, STATE_AXIS)
    margin = HALO * LANE

    pieces, connectivity, potential = lax.optimization_barrier(
        (quarters(block, slots), connectivity, potential)
    )
    pieces = lax.all_to_all(pieces, STATE_AXIS, 0, 0)
    window = pieces.reshape(-1, pieces.shape[2])

    stride = 3 * LANE // QUAD
    local = connectivity - (jnp.arange(cells, dtype=jnp.int32) * stride + ABSENT)[None, :]
    lines = jnp.stack([local.astype(jnp.float32).T, potential.T])
    lines = jnp.pad(lines, ((0, 0), (0, 0), (0, LANE - nodes)))
    near = NEAR * QUAD
    send = jnp.where(slot < slots // 2, lines[:, cells - near :], lines[:, :near])
    route = []
    for i in range(slabs - 1):
        for j in range(slots):
            lower, upper = slots * i + j, slots * (i + 1) + j
            route.append((lower, upper) if j < slots // 2 else (upper, lower))
    other = lax.ppermute(send, everyone, route)
    blank = jnp.zeros((2, LANE - near, LANE), jnp.float32)
    other = jnp.concatenate([other, blank], axis=1)
    lines = jnp.concatenate([lines, other], axis=1)
    columns = jnp.pad(local.astype(jnp.float32), ((0, LANE - nodes), (0, 0)))
    columns = jnp.concatenate([columns, other[0].T], axis=1)
    matrix = jnp.pad(cell_matrix.T, ((0, LANE - nodes), (0, LANE - nodes)))
    matrix = jnp.kron(jnp.eye(2, dtype=matrix.dtype), matrix)

    first, last = window[:, margin : 2 * margin], window[:, -2 * margin : -margin]
    borders = [(slots * i - 1, slots * i) for i in range(1, slabs)]
    borders += [(upper, lower) for lower, upper in borders]
    swapped = lax.ppermute(jnp.where(slot == 0, first, last), everyone, borders)
    second, gram = filtered(window, swapped, lines, columns, matrix)
    parts = gathered_terms(gram)
    orthonormal, factor = orthonormalized(parts, second, block.shape[1] * slabs)
    pieces = orthonormal.reshape(slots, -1, orthonormal.shape[1])
    pieces = lax.all_to_all(pieces, STATE_AXIS, 0, 0)
    return (joined(pieces), factor)


def solution(mesh):
    fine = Mesh(mesh.devices.reshape(SIZES), (*NODE_AXES, STATE_AXIS))
    return jax.shard_map(
        per_device,
        mesh=fine,
        in_specs=(P(STATE_AXIS, NODE_AXES), P(None, NODE_AXES), P(None, NODE_AXES), P()),
        out_specs=(P(STATE_AXIS, NODE_AXES), P()),
        check_vma=False,
    )
```

```python
import functools

import jax
import jax.numpy as jnp
from jax import lax
from jax.experimental import pallas as pl
from jax.experimental.pallas import tpu as pltpu
from jax.sharding import Mesh
from jax.sharding import PartitionSpec as P

CENTER = 3.0
HALF_WIDTH = 3.0
LANE = 128
QUAD = 4
HALO = 6
SPARE = 2
NEAR = 24
ABSENT = 1024
CELL_TILES = ((0, 1), (0, 1, 2), (1, 2), (2, 3))
NODE_AXES = ("z", "y", "core")
STATE_AXIS = "x"
SIZES = (8, 4, 2, 4)
VMEM = pl.BlockSpec(memory_space=pltpu.VMEM)


def floor_div3(x):
    return (x + 999) // 3 - 333


def families(tiles):
    slots = lax.axis_size(STATE_AXIS)
    slot = lax.axis_index(STATE_AXIS)
    edge = tiles
    groups = slots * tiles // 2
    before = slot < slots // 2
    shift = jnp.where(before, groups - NEAR, 0)
    origin = jnp.where(before, -edge - slots * tiles, slots * tiles - edge) - tiles * slot
    return (
        (-edge - tiles * slot, 0, groups),
        (origin + 3 * shift, groups * QUAD, NEAR),
    )


def span(family, low, high):
    origin, line, groups = family
    start = jnp.maximum(-floor_div3(origin - low), 0)
    stop = jnp.minimum(floor_div3(high - origin), groups - 1)
    return line + QUAD * start, origin + 3 * start, jnp.maximum(stop - start + 1, 0)


def group_block(source, origin, acc, cells_ref, columns_ref, matrix_ref, segments):
    down = lax.broadcasted_iota(jnp.int32, (LANE, LANE), 0)
    down = down.astype(jnp.float32).astype(jnp.bfloat16)
    lane = lax.broadcasted_iota(jnp.int32, (16, LANE), 1)
    targets = {}
    for cell in range(QUAD):
        for t in CELL_TILES[cell]:
            row = (lane + (128 * t - 96 * cell)).astype(jnp.float32).astype(jnp.bfloat16)
            targets[cell, t] = jnp.concatenate([row] * (LANE // 16), axis=0)
    one = jnp.ones((LANE, LANE), jnp.bfloat16)
    none = jnp.zeros((LANE, LANE), jnp.bfloat16)
    states, width = source.shape
    sums = [[None] * (3 * len(lines) + 1) for tile, lines in segments]
    groups = [
        (index, part, tile, line)
        for index, (tile, lines) in enumerate(segments)
        for part, line in enumerate(lines)
    ]

    def shift(cell, t):
        return 96.0 * cell - 128.0 * t + ABSENT

    def gather(index, part, tile, line):
        at = jnp.clip((tile + origin + 3 * part) * LANE, 0, width - 4 * LANE)
        x = source[:, pl.ds(pl.multiple_of(at, LANE), 4 * LANE)]
        pickers = []
        for cell in range(QUAD):
            node = cells_ref[0, pl.ds(line + cell, 1), :]
            picked = {}
            for t in CELL_TILES[cell]:
                row = jnp.broadcast_to(node + shift(cell, t), (16, LANE)).astype(jnp.bfloat16)
                row = jnp.concatenate([row] * (LANE // 16), axis=0)
                picked[t] = jnp.where(down == row, one, none)
            pickers.append(picked)
        values = []
        for cell, touched in enumerate(CELL_TILES):
            weights = jnp.concatenate([pickers[cell][t] for t in touched], axis=0)
            x_part = x[:, touched[0] * LANE : (touched[-1] + 1) * LANE]
            values.append(jnp.dot(x_part, weights, preferred_element_type=jnp.float32))
        return values

    def mix(values, index, part, tile, line):
        half = jnp.concatenate([v.astype(jnp.bfloat16) for v in values], axis=0)
        mixed = jnp.dot(half, matrix_ref[...], preferred_element_type=jnp.float32)
        terms = []
        for cell in range(QUAD):
            level = cells_ref[1, pl.ds(line + cell, 1), :]
            term = mixed[states * cell : states * (cell + 1)] + level * values[cell]
            terms.append(term.astype(jnp.bfloat16))
        return terms

    def scatter(terms, index, part, tile, line):
        begin = pl.multiple_of(line // LANE * LANE, LANE)
        columns = columns_ref[:, pl.ds(begin, LANE)]
        placers = []
        for cell in range(QUAD):
            lanes = jnp.full((8, LANE), line - begin + cell, jnp.int32)
            node = jnp.concatenate(
                [
                    jnp.take_along_axis(columns[k : k + 8], lanes, axis=1)
                    for k in range(0, LANE, 8)
                ],
                axis=0,
            )
            node = (node + ABSENT).astype(jnp.bfloat16)
            placers.append(
                {t: jnp.where(node == targets[cell, t], one, none) for t in CELL_TILES[cell]}
            )
        for begin, cells in ((0, (0, 1, 2)), (2, (1, 2, 3))):
            weights = jnp.concatenate(
                [
                    jnp.concatenate([placers[c].get(t, none) for t in (begin, begin + 1)], axis=1)
                    for c in cells
                ],
                axis=0,
            )
            spread = jnp.dot(
                jnp.concatenate([terms[c] for c in cells], axis=1),
                weights,
                preferred_element_type=jnp.float32,
            )
            for i in range(2):
                k = 3 * part + begin + i
                piece = spread[:, i * LANE : (i + 1) * LANE]
                total = sums[index][k]
                sums[index][k] = piece if total is None else total + piece
        lines = segments[index][1]
        for k in range(3 * part, 3 * part + (4 if part == len(lines) - 1 else 3)):
            at = pl.multiple_of((tile + HALO + k) * LANE, LANE)
            acc[:, pl.ds(at, LANE)] += sums[index][k]

    values, terms = {}, {}
    for step in range(len(groups) + 2):
        if step < len(groups):
            values[step] = gather(*groups[step])
        if 0 <= step - 1 < len(groups):
            terms[step - 1] = mix(values.pop(step - 1), *groups[step - 1])
        if 0 <= step - 2:
            scatter(terms.pop(step - 2), *groups[step - 2])


def lines_of(line, count, parts, blank):
    return [jnp.where(i < count, line + QUAD * i, blank) for i in range(parts)]


def segment(family, low, high, parts, blank):
    line, tile, count = span(family, low, high)
    return jnp.clip(tile, low, low + 3), lines_of(line, count, parts, blank)


def interior_kernel(window_ref, cells_ref, columns_ref, matrix_ref, acc_ref):
    states, whole = window_ref.shape
    tiles = whole // LANE - 2 * HALO
    blank = cells_ref.shape[1] - QUAD
    acc_ref[:, pl.ds(0, whole)] = jnp.zeros((states, whole), jnp.float32)
    parts = (tiles - 1) // 3
    inner = [segment(f, 0, tiles - 4, parts, blank) for f in families(tiles)]
    group_block(window_ref, HALO, acc_ref, cells_ref, columns_ref, matrix_ref, inner)


def rest_kernel(
    swapped_ref,
    cells_ref,
    columns_ref,
    matrix_ref,
    acc_ref,
    window_ref,
    second_ref,
    gram_ref,
    field,
    acc,
):
    states, owned = second_ref.shape
    tiles = owned // LANE
    margin = HALO * LANE
    blank = cells_ref.shape[1] - QUAD
    slot = lax.axis_index(STATE_AXIS)
    slab = lax.axis_index(NODE_AXES[0])
    slabs = lax.axis_size(NODE_AXES[0])
    for axis in NODE_AXES[1:]:
        slab = slab * lax.axis_size(axis) + lax.axis_index(axis)
        slabs = slabs * lax.axis_size(axis)
    whole = owned + 2 * margin
    field[...] = window_ref[...]
    acc[:, pl.ds(0, whole)] = jnp.zeros((states, whole), jnp.float32)

    @pl.when(slot == 0)
    def _():
        field[:, pl.ds(0, margin)] = swapped_ref[...]

    @pl.when(slot == lax.axis_size(STATE_AXIS) - 1)
    def _():
        field[:, pl.ds(margin + owned, margin)] = swapped_ref[...]


    ends = [
        segment(family, low, low + HALO - 1, 2, blank)
        for low in (-HALO, tiles - 3)
        for family in families(tiles)
    ]
    group_block(field, HALO, acc, cells_ref, columns_ref, matrix_ref, ends)

    chunk = 4 * LANE

    def to_first(step, carry):
        here = pl.ds(pl.multiple_of(step * chunk, LANE), chunk)
        start = field[:, here].astype(jnp.float32)
        image = acc_ref[:, here] + acc[:, here] - CENTER * start
        field[:, here] = (image * (1.0 / HALF_WIDTH)).astype(field.dtype)
        acc[:, here] = jnp.zeros((states, chunk), jnp.float32)
        return carry

    lax.fori_loop(0, whole // chunk, to_first, 0)

    @pl.when((slab == 0) & (slot == 0))
    def _():
        field[:, pl.ds(0, margin)] = jnp.zeros((states, margin), field.dtype)

    @pl.when((slab == slabs - 1) & (slot == lax.axis_size(STATE_AXIS) - 1))
    def _():
        field[:, pl.ds(margin + owned, margin)] = jnp.zeros((states, margin), field.dtype)

    parts = (tiles + 2) // 3
    own, other = families(tiles)
    whole_range = [
        segment(own, -3, tiles - 1, parts + 1, blank),
        segment(other, -3, tiles - 1, parts, blank),
    ]
    group_block(field, HALO, acc, cells_ref, columns_ref, matrix_ref, whole_range)

    chunk = 16 * LANE

    def to_second(step, gram):
        at = pl.multiple_of(step * chunk, LANE)
        here = pl.ds(pl.multiple_of(at + margin, LANE), chunk)
        image = acc[:, here] - CENTER * field[:, here].astype(jnp.float32)
        start = window_ref[:, here].astype(jnp.float32)
        second = (image * (2.0 / HALF_WIDTH) - start).astype(second_ref.dtype)
        second_ref[:, pl.ds(at, chunk)] = second
        return gram + lax.dot_general(
            second, second, (((1,), (1,)), ((), ())), preferred_element_type=jnp.float32
        )

    gram = lax.fori_loop(0, owned // chunk, to_second, jnp.zeros((states, states), jnp.float32))
    gram_ref[...] = jnp.concatenate([gram[: states // 2], gram[states // 2 :]], axis=1)


def filtered(window, swapped, cells, columns, matrix):
    states, width = window.shape
    count = width - 2 * HALO * LANE
    total = jax.ShapeDtypeStruct((states, width + SPARE * LANE), jnp.float32)
    params = pltpu.CompilerParams(vmem_limit_bytes=24 << 20)
    acc = pl.pallas_call(
        interior_kernel,
        out_shape=total,
        in_specs=[VMEM] * 4,
        out_specs=VMEM,
        compiler_params=params,
        cost_estimate=pl.CostEstimate(
            flops=20_000_000_000, bytes_accessed=20_000_000, transcendentals=0
        ),
        name="interior",
    )(window, cells, columns, matrix)
    return pl.pallas_call(
        rest_kernel,
        out_shape=(
            jax.ShapeDtypeStruct((states, count), window.dtype),
            jax.ShapeDtypeStruct((states // 2, 2 * states), jnp.float32),
        ),
        in_specs=[VMEM] * 6,
        out_specs=[VMEM] * 2,
        scratch_shapes=[
            pltpu.VMEM(window.shape, window.dtype),
            pltpu.VMEM(total.shape, total.dtype),
        ],
        compiler_params=params,
        name="rest",
    )(swapped, cells, columns, matrix, acc, window)


def factor_kernel(total_nodes, parts_ref, second_ref, orthonormal_ref, factor_ref):
    states, owned = second_ref.shape
    packed = parts_ref[0]
    for i in range(1, parts_ref.shape[0]):
        packed = packed + parts_ref[i]
    packed = packed * (1.0 / total_nodes)
    matrix = jnp.concatenate([packed[:, :states], packed[:, states:]], axis=0)
    row_of = lax.broadcasted_iota(jnp.int32, (states, states), 0)
    col_of = lax.broadcasted_iota(jnp.int32, (states, states), 1)
    identity = jnp.where(row_of == col_of, 1.0, 0.0)
    both = jnp.concatenate([matrix, identity], axis=1)
    tall = 8
    shape = (tall, 2 * states)
    bands = [both[tall * k : tall * (k + 1)] for k in range(states // tall)]
    within = lax.broadcasted_iota(jnp.int32, shape, 0)
    for k in range(len(bands)):
        later = bands[k + 1 :]
        rows = [jnp.broadcast_to(bands[k][i : i + 1], shape) for i in range(tall)]

        def replicated(values, i):
            return jnp.broadcast_to(values[:, tall * k + i : tall * k + i + 1], shape)

        pivot = {(i, l): replicated(rows[i], l) for i in range(tall) for l in range(i, tall)}
        columns = [[replicated(band, i) for band in later] for i in range(tall)]
        done = jnp.zeros(shape, jnp.float32)
        for i in range(tall):
            inverse = 1.0 / pivot[i, i]
            scaled = rows[i] * inverse
            done = jnp.where(within == i, rows[i] * lax.rsqrt(pivot[i, i]), done)
            later = [band - c * scaled for band, c in zip(later, columns[i])]
            for m in range(i + 1, tall):
                ratio = pivot[i, m] * inverse
                rows[m] = rows[m] - pivot[i, m] * scaled
                for l in range(m, tall):
                    pivot[m, l] = pivot[m, l] - ratio * pivot[i, l]
                columns[m] = [c - d * ratio for c, d in zip(columns[m], columns[i])]
        bands[k:] = [done, *later]
    both = jnp.concatenate(bands, axis=0)
    left = jnp.where(col_of >= row_of, both[:, :states], 0.0)
    factor_ref[...] = left.T
    inverse = both[:, states:].astype(jnp.bfloat16)
    chunk = 16 * LANE

    def body(step, carry):
        here = pl.ds(pl.multiple_of(step * chunk, LANE), chunk)
        orthonormal_ref[:, here] = jnp.dot(
            inverse, second_ref[:, here], preferred_element_type=jnp.float32
        ).astype(orthonormal_ref.dtype)
        return carry

    lax.fori_loop(0, owned // chunk, body, 0)


def orthonormalized(parts, second, total_nodes):
    states = second.shape[0]
    return pl.pallas_call(
        functools.partial(factor_kernel, total_nodes),
        out_shape=(
            jax.ShapeDtypeStruct(second.shape, second.dtype),
            jax.ShapeDtypeStruct((states, states), jnp.float32),
        ),
        in_specs=[VMEM] * 2,
        out_specs=[VMEM] * 2,
        compiler_params=pltpu.CompilerParams(vmem_limit_bytes=8 << 20),
        name="factor",
    )(parts, second)


def split_kernel(block_ref, pieces_ref, held, came, went):
    count, states, width = pieces_ref.shape
    total = block_ref.shape[1]
    margin = HALO * LANE
    owned = total // count
    tall, wide = 8, total // 2
    arriving = [(row, at) for row in range(0, states, tall) for at in range(0, total, wide)]
    leaving = []
    for row in range(0, states, tall):
        for i in range(count):
            begin, place, size = owned * i - margin, 0, width
            if i == 0:
                leaving.append((i, row, 0, 0, margin))
                begin, place, size = 0, margin, size - margin
            if i == count - 1:
                leaving.append((i, row, total - margin, width - margin, margin))
                size -= margin
            leaving.append((i, row, begin, place, size))

    def copy_in(k):
        row, at = arriving[k]
        part = (pl.ds(row, tall), pl.ds(at, wide))
        return pltpu.make_async_copy(block_ref.at[part], held.at[part], came.at[k])

    def copy_out(k):
        i, row, column, place, size = leaving[k]
        source = held.at[pl.ds(row, tall), pl.ds(column, size)]
        target = pieces_ref.at[i, pl.ds(row, tall), pl.ds(place, size)]
        return pltpu.make_async_copy(source, target, went.at[k])

    for k in range(len(arriving)):
        copy_in(k).start()
    left = list(range(len(leaving)))
    for k, (row, at) in enumerate(arriving):
        copy_in(k).wait()
        for j in list(left):
            i, state, column, place, size = leaving[j]
            if state < row or (state == row and column + size <= at + wide):
                copy_out(j).start()
                left.remove(j)
    for k in range(len(leaving)):
        copy_out(k).wait()


def join_kernel(pieces_ref, block_ref, done):
    copies = []
    for i in range(pieces_ref.shape[0]):
        width = pieces_ref.shape[2]
        part = block_ref.at[:, pl.ds(i * width, width)]
        copies.append(pltpu.make_async_copy(pieces_ref.at[i], part, done.at[i]))
        copies[-1].start()
    for copy in copies:
        copy.wait()


def quarters(block, count):
    states, total = block.shape
    shape = (count, states, total // count + 2 * HALO * LANE)
    return pl.pallas_call(
        split_kernel,
        out_shape=jax.ShapeDtypeStruct(shape, block.dtype),
        in_specs=[pl.BlockSpec(memory_space=pltpu.HBM)],
        out_specs=pl.BlockSpec(memory_space=pltpu.HBM),
        scratch_shapes=[
            pltpu.VMEM(block.shape, block.dtype),
            pltpu.SemaphoreType.DMA((states // 4,)),
            pltpu.SemaphoreType.DMA((states // 8 * (count + 2),)),
        ],
        name="quarters",
    )(block)


def joined(pieces):
    count, states, width = pieces.shape
    return pl.pallas_call(
        join_kernel,
        out_shape=jax.ShapeDtypeStruct((states, count * width), pieces.dtype),
        in_specs=[VMEM],
        out_specs=pl.BlockSpec(memory_space=pl.ANY),
        scratch_shapes=[pltpu.SemaphoreType.DMA((count,))],
        compiler_params=pltpu.CompilerParams(vmem_limit_bytes=4 << 20),
        name="joined",
    )(pieces)


def gathered_terms(x):
    x = x + lax.ppermute(x, "core", [(0, 1), (1, 0)])
    group = ("y", "x")
    size = lax.axis_size("y") * lax.axis_size("x")
    x = lax.all_to_all(jnp.broadcast_to(x[None], (size, *x.shape)), group, 0, 0).sum(0)
    copies = jnp.broadcast_to(x[None], (lax.axis_size("z"), *x.shape))
    return lax.all_to_all(copies, "z", 0, 0)


def per_device(block, connectivity, potential, cell_matrix):
    nodes, cells = connectivity.shape
    slots = lax.axis_size(STATE_AXIS)
    slot = lax.axis_index(STATE_AXIS)
    slabs = lax.axis_size(NODE_AXES)
    everyone = (*NODE_AXES, STATE_AXIS)
    margin = HALO * LANE

    pieces, connectivity, potential = lax.optimization_barrier(
        (quarters(block, slots), connectivity, potential)
    )
    pieces = lax.all_to_all(pieces, STATE_AXIS, 0, 0)
    window = pieces.reshape(-1, pieces.shape[2])

    stride = 3 * LANE // QUAD
    local = connectivity - (jnp.arange(cells, dtype=jnp.int32) * stride + ABSENT)[None, :]
    lines = jnp.stack([local.astype(jnp.float32).T, potential.T])
    lines = jnp.pad(lines, ((0, 0), (0, 0), (0, LANE - nodes)))
    near = NEAR * QUAD
    send = jnp.where(slot < slots // 2, lines[:, cells - near :], lines[:, :near])
    route = []
    for i in range(slabs - 1):
        for j in range(slots):
            lower, upper = slots * i + j, slots * (i + 1) + j
            route.append((lower, upper) if j < slots // 2 else (upper, lower))
    other = lax.ppermute(send, everyone, route)
    blank = jnp.zeros((2, LANE - near, LANE), jnp.float32)
    other = jnp.concatenate([other, blank], axis=1)
    lines = jnp.concatenate([lines, other], axis=1)
    columns = jnp.pad(local.astype(jnp.float32), ((0, LANE - nodes), (0, 0)))
    columns = jnp.concatenate([columns, other[0].T], axis=1)
    matrix = jnp.pad(cell_matrix.T, ((0, LANE - nodes), (0, LANE - nodes)))

    first, last = window[:, margin : 2 * margin], window[:, -2 * margin : -margin]
    borders = [(slots * i - 1, slots * i) for i in range(1, slabs)]
    borders += [(upper, lower) for lower, upper in borders]
    swapped = lax.ppermute(jnp.where(slot == 0, first, last), everyone, borders)
    second, gram = filtered(window, swapped, lines, columns, matrix)
    parts = gathered_terms(gram)
    orthonormal, factor = orthonormalized(parts, second, block.shape[1] * slabs)
    pieces = orthonormal.reshape(slots, -1, orthonormal.shape[1])
    pieces = lax.all_to_all(pieces, STATE_AXIS, 0, 0)
    return (joined(pieces), factor)


def solution(mesh):
    fine = Mesh(mesh.devices.reshape(SIZES), (*NODE_AXES, STATE_AXIS))
    return jax.shard_map(
        per_device,
        mesh=fine,
        in_specs=(P(STATE_AXIS, NODE_AXES), P(None, NODE_AXES), P(None, NODE_AXES), P()),
        out_specs=(P(STATE_AXIS, NODE_AXES), P()),
        check_vma=False,
    )
```

```python
import functools

import jax
import jax.numpy as jnp
from jax import lax
from jax.experimental import pallas as pl
from jax.experimental.pallas import tpu as pltpu
from jax.sharding import Mesh
from jax.sharding import PartitionSpec as P

CENTER = 3.0
HALF_WIDTH = 3.0
LANE = 128
QUAD = 4
HALO = 6
SPARE = 2
NEAR = 24
ABSENT = 1024
CELL_TILES = ((0, 1), (0, 1, 2), (1, 2), (2, 3))
NODE_AXES = ("z", "y", "core")
STATE_AXIS = "x"
SIZES = (8, 4, 2, 4)
VMEM = pl.BlockSpec(memory_space=pltpu.VMEM)


def floor_div3(x):
    return (x + 999) // 3 - 333


def families(tiles):
    slots = lax.axis_size(STATE_AXIS)
    slot = lax.axis_index(STATE_AXIS)
    edge = tiles
    groups = slots * tiles // 2
    before = slot < slots // 2
    shift = jnp.where(before, groups - NEAR, 0)
    origin = jnp.where(before, -edge - slots * tiles, slots * tiles - edge) - tiles * slot
    return (
        (-edge - tiles * slot, 0, groups),
        (origin + 3 * shift, groups * QUAD, NEAR),
    )


def span(family, low, high):
    origin, line, groups = family
    start = jnp.maximum(-floor_div3(origin - low), 0)
    stop = jnp.minimum(floor_div3(high - origin), groups - 1)
    return line + QUAD * start, origin + 3 * start, jnp.maximum(stop - start + 1, 0)


def group_block(source, origin, acc, cells_ref, columns_ref, matrix_ref, segments):
    down = lax.broadcasted_iota(jnp.int32, (LANE, LANE), 0)
    down = down.astype(jnp.float32).astype(jnp.bfloat16)
    lane = lax.broadcasted_iota(jnp.int32, (16, LANE), 1)
    targets = {}
    for cell in range(QUAD):
        for t in CELL_TILES[cell]:
            row = (lane + (128 * t - 96 * cell)).astype(jnp.float32).astype(jnp.bfloat16)
            targets[cell, t] = jnp.concatenate([row] * (LANE // 16), axis=0)
    one = jnp.ones((LANE, LANE), jnp.bfloat16)
    none = jnp.zeros((LANE, LANE), jnp.bfloat16)
    states, width = source.shape
    sums = [[None] * (3 * len(lines) + 1) for tile, lines in segments]
    groups = [
        (index, part, tile, line)
        for index, (tile, lines) in enumerate(segments)
        for part, line in enumerate(lines)
    ]

    def shift(cell, t):
        return 96.0 * cell - 128.0 * t + ABSENT

    def gather(index, part, tile, line):
        at = jnp.clip((tile + origin + 3 * part) * LANE, 0, width - 4 * LANE)
        x = source[:, pl.ds(pl.multiple_of(at, LANE), 4 * LANE)]
        pickers = []
        for cell in range(QUAD):
            node = cells_ref[0, pl.ds(line + cell, 1), :]
            picked = {}
            for t in CELL_TILES[cell]:
                row = jnp.broadcast_to(node + shift(cell, t), (16, LANE)).astype(jnp.bfloat16)
                row = jnp.concatenate([row] * (LANE // 16), axis=0)
                picked[t] = jnp.where(down == row, one, none)
            pickers.append(picked)
        values = []
        for cell, touched in enumerate(CELL_TILES):
            weights = jnp.concatenate([pickers[cell][t] for t in touched], axis=0)
            x_part = x[:, touched[0] * LANE : (touched[-1] + 1) * LANE]
            values.append(jnp.dot(x_part, weights, preferred_element_type=jnp.float32))
        return values

    def mix(values, index, part, tile, line):
        half = jnp.concatenate([v.astype(jnp.bfloat16) for v in values], axis=0)
        mixed = jnp.dot(half, matrix_ref[...], preferred_element_type=jnp.float32)
        terms = []
        for cell in range(QUAD):
            level = cells_ref[1, pl.ds(line + cell, 1), :]
            term = mixed[states * cell : states * (cell + 1)] + level * values[cell]
            terms.append(term.astype(jnp.bfloat16))
        return terms

    def scatter(terms, index, part, tile, line):
        begin = pl.multiple_of(line // LANE * LANE, LANE)
        columns = columns_ref[:, pl.ds(begin, LANE)]
        placers = []
        for cell in range(QUAD):
            lanes = jnp.full((8, LANE), line - begin + cell, jnp.int32)
            node = jnp.concatenate(
                [
                    jnp.take_along_axis(columns[k : k + 8], lanes, axis=1)
                    for k in range(0, LANE, 8)
                ],
                axis=0,
            )
            node = (node + ABSENT).astype(jnp.bfloat16)
            placers.append(
                {t: jnp.where(node == targets[cell, t], one, none) for t in CELL_TILES[cell]}
            )
        for begin, cells in ((0, (0, 1, 2)), (2, (1, 2, 3))):
            weights = jnp.concatenate(
                [
                    jnp.concatenate([placers[c].get(t, none) for t in (begin, begin + 1)], axis=1)
                    for c in cells
                ],
                axis=0,
            )
            spread = jnp.dot(
                jnp.concatenate([terms[c] for c in cells], axis=1),
                weights,
                preferred_element_type=jnp.float32,
            )
            for i in range(2):
                k = 3 * part + begin + i
                piece = spread[:, i * LANE : (i + 1) * LANE]
                total = sums[index][k]
                sums[index][k] = piece if total is None else total + piece
        lines = segments[index][1]
        for k in range(3 * part, 3 * part + (4 if part == len(lines) - 1 else 3)):
            at = pl.multiple_of((tile + HALO + k) * LANE, LANE)
            acc[:, pl.ds(at, LANE)] += sums[index][k]

    values, terms = {}, {}
    for step in range(len(groups) + 2):
        if step < len(groups):
            values[step] = gather(*groups[step])
        if 0 <= step - 1 < len(groups):
            terms[step - 1] = mix(values.pop(step - 1), *groups[step - 1])
        if 0 <= step - 2:
            scatter(terms.pop(step - 2), *groups[step - 2])


def lines_of(line, count, parts, blank):
    return [jnp.where(i < count, line + QUAD * i, blank) for i in range(parts)]


def segment(family, low, high, parts, blank):
    line, tile, count = span(family, low, high)
    return jnp.clip(tile, low, low + 3), lines_of(line, count, parts, blank)


def interior_kernel(window_ref, cells_ref, columns_ref, matrix_ref, acc_ref):
    states, whole = window_ref.shape
    tiles = whole // LANE - 2 * HALO
    blank = cells_ref.shape[1] - QUAD
    acc_ref[:, pl.ds(0, whole)] = jnp.zeros((states, whole), jnp.float32)
    parts = (tiles - 1) // 3
    inner = [segment(f, 0, tiles - 4, parts, blank) for f in families(tiles)]
    group_block(window_ref, HALO, acc_ref, cells_ref, columns_ref, matrix_ref, inner)


def rest_kernel(
    swapped_ref,
    cells_ref,
    columns_ref,
    matrix_ref,
    acc_ref,
    window_ref,
    second_ref,
    gram_ref,
    field,
    acc,
):
    states, owned = second_ref.shape
    tiles = owned // LANE
    margin = HALO * LANE
    blank = cells_ref.shape[1] - QUAD
    slot = lax.axis_index(STATE_AXIS)
    slab = lax.axis_index(NODE_AXES[0])
    slabs = lax.axis_size(NODE_AXES[0])
    for axis in NODE_AXES[1:]:
        slab = slab * lax.axis_size(axis) + lax.axis_index(axis)
        slabs = slabs * lax.axis_size(axis)
    whole = owned + 2 * margin
    field[...] = window_ref[...]
    reach = 2 * margin
    for begin in (0, whole - reach):
        acc[:, pl.ds(begin, reach)] = jnp.zeros((states, reach), jnp.float32)

    @pl.when(slot == 0)
    def _():
        field[:, pl.ds(0, margin)] = swapped_ref[...]

    @pl.when(slot == lax.axis_size(STATE_AXIS) - 1)
    def _():
        field[:, pl.ds(margin + owned, margin)] = swapped_ref[...]


    ends = [
        segment(family, low, low + HALO - 1, 2, blank)
        for low in (-HALO, tiles - 3)
        for family in families(tiles)
    ]
    group_block(field, HALO, acc, cells_ref, columns_ref, matrix_ref, ends)

    chunk = 4 * LANE

    def to_first(near, step, carry):
        here = pl.ds(pl.multiple_of(step * chunk, LANE), chunk)
        start = field[:, here].astype(jnp.float32)
        image = acc_ref[:, here] - CENTER * start
        if near:
            image = image + acc[:, here]
        field[:, here] = (image * (1.0 / HALF_WIDTH)).astype(field.dtype)
        acc[:, here] = jnp.zeros((states, chunk), jnp.float32)
        return carry

    steps, ends_steps = whole // chunk, reach // chunk
    lax.fori_loop(0, ends_steps, functools.partial(to_first, True), 0)
    lax.fori_loop(ends_steps, steps - ends_steps, functools.partial(to_first, False), 0)
    lax.fori_loop(steps - ends_steps, steps, functools.partial(to_first, True), 0)

    @pl.when((slab == 0) & (slot == 0))
    def _():
        field[:, pl.ds(0, margin)] = jnp.zeros((states, margin), field.dtype)

    @pl.when((slab == slabs - 1) & (slot == lax.axis_size(STATE_AXIS) - 1))
    def _():
        field[:, pl.ds(margin + owned, margin)] = jnp.zeros((states, margin), field.dtype)

    parts = (tiles + 2) // 3
    own, other = families(tiles)
    whole_range = [
        segment(own, -3, tiles - 1, parts + 1, blank),
        segment(other, -3, tiles - 1, parts, blank),
    ]
    group_block(field, HALO, acc, cells_ref, columns_ref, matrix_ref, whole_range)

    chunk = 32 * LANE

    def to_second(step, gram):
        at = pl.multiple_of(step * chunk, LANE)
        here = pl.ds(pl.multiple_of(at + margin, LANE), chunk)
        image = acc[:, here] - CENTER * field[:, here].astype(jnp.float32)
        start = window_ref[:, here].astype(jnp.float32)
        second = (image * (2.0 / HALF_WIDTH) - start).astype(second_ref.dtype)
        second_ref[:, pl.ds(at, chunk)] = second
        return gram + lax.dot_general(
            second, second, (((1,), (1,)), ((), ())), preferred_element_type=jnp.float32
        )

    gram = lax.fori_loop(0, owned // chunk, to_second, jnp.zeros((states, states), jnp.float32))
    gram_ref[...] = jnp.concatenate([gram[: states // 2], gram[states // 2 :]], axis=1)


def filtered(window, swapped, cells, columns, matrix):
    states, width = window.shape
    count = width - 2 * HALO * LANE
    total = jax.ShapeDtypeStruct((states, width + SPARE * LANE), jnp.float32)
    params = pltpu.CompilerParams(vmem_limit_bytes=24 << 20)
    acc = pl.pallas_call(
        interior_kernel,
        out_shape=total,
        in_specs=[VMEM] * 4,
        out_specs=VMEM,
        compiler_params=params,
        cost_estimate=pl.CostEstimate(
            flops=20_000_000_000, bytes_accessed=20_000_000, transcendentals=0
        ),
        name="interior",
    )(window, cells, columns, matrix)
    return pl.pallas_call(
        rest_kernel,
        out_shape=(
            jax.ShapeDtypeStruct((states, count), window.dtype),
            jax.ShapeDtypeStruct((states // 2, 2 * states), jnp.float32),
        ),
        in_specs=[VMEM] * 6,
        out_specs=[VMEM] * 2,
        scratch_shapes=[
            pltpu.VMEM(window.shape, window.dtype),
            pltpu.VMEM(total.shape, total.dtype),
        ],
        compiler_params=params,
        name="rest",
    )(swapped, cells, columns, matrix, acc, window)


def factor_kernel(total_nodes, parts_ref, second_ref, orthonormal_ref, factor_ref):
    states, owned = second_ref.shape
    packed = parts_ref[0]
    for i in range(1, parts_ref.shape[0]):
        packed = packed + parts_ref[i]
    packed = packed * (1.0 / total_nodes)
    matrix = jnp.concatenate([packed[:, :states], packed[:, states:]], axis=0)
    row_of = lax.broadcasted_iota(jnp.int32, (states, states), 0)
    col_of = lax.broadcasted_iota(jnp.int32, (states, states), 1)
    identity = jnp.where(row_of == col_of, 1.0, 0.0)
    both = jnp.concatenate([matrix, identity], axis=1)
    tall = 8
    shape = (tall, 2 * states)
    bands = [both[tall * k : tall * (k + 1)] for k in range(states // tall)]
    within = lax.broadcasted_iota(jnp.int32, shape, 0)
    for k in range(len(bands)):
        later = bands[k + 1 :]
        rows = [jnp.broadcast_to(bands[k][i : i + 1], shape) for i in range(tall)]

        def replicated(values, i):
            return jnp.broadcast_to(values[:, tall * k + i : tall * k + i + 1], shape)

        pivot = {(i, l): replicated(rows[i], l) for i in range(tall) for l in range(i, tall)}
        columns = [[replicated(band, i) for band in later] for i in range(tall)]
        done = jnp.zeros(shape, jnp.float32)
        for i in range(tall):
            inverse = 1.0 / pivot[i, i]
            scaled = rows[i] * inverse
            done = jnp.where(within == i, rows[i] * lax.rsqrt(pivot[i, i]), done)
            later = [band - c * scaled for band, c in zip(later, columns[i])]
            for m in range(i + 1, tall):
                ratio = pivot[i, m] * inverse
                rows[m] = rows[m] - pivot[i, m] * scaled
                for l in range(m, tall):
                    pivot[m, l] = pivot[m, l] - ratio * pivot[i, l]
                columns[m] = [c - d * ratio for c, d in zip(columns[m], columns[i])]
        bands[k:] = [done, *later]
    both = jnp.concatenate(bands, axis=0)
    left = jnp.where(col_of >= row_of, both[:, :states], 0.0)
    factor_ref[...] = left.T
    inverse = both[:, states:].astype(jnp.bfloat16)
    chunk = 16 * LANE

    def body(step, carry):
        here = pl.ds(pl.multiple_of(step * chunk, LANE), chunk)
        orthonormal_ref[:, here] = jnp.dot(
            inverse, second_ref[:, here], preferred_element_type=jnp.float32
        ).astype(orthonormal_ref.dtype)
        return carry

    lax.fori_loop(0, owned // chunk, body, 0)


def orthonormalized(parts, second, total_nodes):
    states = second.shape[0]
    return pl.pallas_call(
        functools.partial(factor_kernel, total_nodes),
        out_shape=(
            jax.ShapeDtypeStruct(second.shape, second.dtype),
            jax.ShapeDtypeStruct((states, states), jnp.float32),
        ),
        in_specs=[VMEM] * 2,
        out_specs=[VMEM] * 2,
        compiler_params=pltpu.CompilerParams(vmem_limit_bytes=8 << 20),
        name="factor",
    )(parts, second)


def split_kernel(block_ref, pieces_ref, held, came, went):
    count, states, width = pieces_ref.shape
    total = block_ref.shape[1]
    margin = HALO * LANE
    owned = total // count
    tall, wide = 8, total // 2
    arriving = [(row, at) for row in range(0, states, tall) for at in range(0, total, wide)]
    leaving = []
    for row in range(0, states, tall):
        for i in range(count):
            begin, place, size = owned * i - margin, 0, width
            if i == 0:
                leaving.append((i, row, 0, 0, margin))
                begin, place, size = 0, margin, size - margin
            if i == count - 1:
                leaving.append((i, row, total - margin, width - margin, margin))
                size -= margin
            leaving.append((i, row, begin, place, size))

    def copy_in(k):
        row, at = arriving[k]
        part = (pl.ds(row, tall), pl.ds(at, wide))
        return pltpu.make_async_copy(block_ref.at[part], held.at[part], came.at[k])

    def copy_out(k):
        i, row, column, place, size = leaving[k]
        source = held.at[pl.ds(row, tall), pl.ds(column, size)]
        target = pieces_ref.at[i, pl.ds(row, tall), pl.ds(place, size)]
        return pltpu.make_async_copy(source, target, went.at[k])

    for k in range(len(arriving)):
        copy_in(k).start()
    left = list(range(len(leaving)))
    for k, (row, at) in enumerate(arriving):
        copy_in(k).wait()
        for j in list(left):
            i, state, column, place, size = leaving[j]
            if state < row or (state == row and column + size <= at + wide):
                copy_out(j).start()
                left.remove(j)
    for k in range(len(leaving)):
        copy_out(k).wait()


def join_kernel(pieces_ref, block_ref, done):
    copies = []
    for i in range(pieces_ref.shape[0]):
        width = pieces_ref.shape[2]
        part = block_ref.at[:, pl.ds(i * width, width)]
        copies.append(pltpu.make_async_copy(pieces_ref.at[i], part, done.at[i]))
        copies[-1].start()
    for copy in copies:
        copy.wait()


def quarters(block, count):
    states, total = block.shape
    shape = (count, states, total // count + 2 * HALO * LANE)
    return pl.pallas_call(
        split_kernel,
        out_shape=jax.ShapeDtypeStruct(shape, block.dtype),
        in_specs=[pl.BlockSpec(memory_space=pltpu.HBM)],
        out_specs=pl.BlockSpec(memory_space=pltpu.HBM),
        scratch_shapes=[
            pltpu.VMEM(block.shape, block.dtype),
            pltpu.SemaphoreType.DMA((states // 4,)),
            pltpu.SemaphoreType.DMA((states // 8 * (count + 2),)),
        ],
        name="quarters",
    )(block)


def joined(pieces):
    count, states, width = pieces.shape
    return pl.pallas_call(
        join_kernel,
        out_shape=jax.ShapeDtypeStruct((states, count * width), pieces.dtype),
        in_specs=[VMEM],
        out_specs=pl.BlockSpec(memory_space=pl.ANY),
        scratch_shapes=[pltpu.SemaphoreType.DMA((count,))],
        compiler_params=pltpu.CompilerParams(vmem_limit_bytes=4 << 20),
        name="joined",
    )(pieces)


def gathered_terms(x):
    x = x + lax.ppermute(x, "core", [(0, 1), (1, 0)])
    group = ("y", "x")
    size = lax.axis_size("y") * lax.axis_size("x")
    x = lax.all_to_all(jnp.broadcast_to(x[None], (size, *x.shape)), group, 0, 0).sum(0)
    copies = jnp.broadcast_to(x[None], (lax.axis_size("z"), *x.shape))
    return lax.all_to_all(copies, "z", 0, 0)


def per_device(block, connectivity, potential, cell_matrix):
    nodes, cells = connectivity.shape
    slots = lax.axis_size(STATE_AXIS)
    slot = lax.axis_index(STATE_AXIS)
    slabs = lax.axis_size(NODE_AXES)
    everyone = (*NODE_AXES, STATE_AXIS)
    margin = HALO * LANE

    pieces, connectivity, potential = lax.optimization_barrier(
        (quarters(block, slots), connectivity, potential)
    )
    pieces = lax.all_to_all(pieces, STATE_AXIS, 0, 0)
    window = pieces.reshape(-1, pieces.shape[2])

    stride = 3 * LANE // QUAD
    local = connectivity - (jnp.arange(cells, dtype=jnp.int32) * stride + ABSENT)[None, :]
    lines = jnp.stack([local.astype(jnp.float32).T, potential.T])
    lines = jnp.pad(lines, ((0, 0), (0, 0), (0, LANE - nodes)))
    near = NEAR * QUAD
    send = jnp.where(slot < slots // 2, lines[:, cells - near :], lines[:, :near])
    route = []
    for i in range(slabs - 1):
        for j in range(slots):
            lower, upper = slots * i + j, slots * (i + 1) + j
            route.append((lower, upper) if j < slots // 2 else (upper, lower))
    other = lax.ppermute(send, everyone, route)
    blank = jnp.zeros((2, LANE - near, LANE), jnp.float32)
    other = jnp.concatenate([other, blank], axis=1)
    lines = jnp.concatenate([lines, other], axis=1)
    columns = jnp.pad(local.astype(jnp.float32), ((0, LANE - nodes), (0, 0)))
    columns = jnp.concatenate([columns, other[0].T], axis=1)
    matrix = jnp.pad(cell_matrix.T, ((0, LANE - nodes), (0, LANE - nodes)))

    first, last = window[:, margin : 2 * margin], window[:, -2 * margin : -margin]
    borders = [(slots * i - 1, slots * i) for i in range(1, slabs)]
    borders += [(upper, lower) for lower, upper in borders]
    swapped = lax.ppermute(jnp.where(slot == 0, first, last), everyone, borders)
    second, gram = filtered(window, swapped, lines, columns, matrix)
    parts = gathered_terms(gram)
    orthonormal, factor = orthonormalized(parts, second, block.shape[1] * slabs)
    pieces = orthonormal.reshape(slots, -1, orthonormal.shape[1])
    pieces = lax.all_to_all(pieces, STATE_AXIS, 0, 0)
    return (joined(pieces), factor)


def solution(mesh):
    fine = Mesh(mesh.devices.reshape(SIZES), (*NODE_AXES, STATE_AXIS))
    return jax.shard_map(
        per_device,
        mesh=fine,
        in_specs=(P(STATE_AXIS, NODE_AXES), P(None, NODE_AXES), P(None, NODE_AXES), P()),
        out_specs=(P(STATE_AXIS, NODE_AXES), P()),
        check_vma=False,
    )
```
